32 devices in a mesh: groups: 2 (over x), row: 16 (over z, y, core).
Axes of the slice: x: 2, y: 2, z: 4, core: 2. Of those that a mesh axis runs over, the one named last changes fastest.
Arguments:
- pair: bfloat16 [256, 128, 128], P(('groups', 'row')), parts along dimension 0, may hold values from -6 to 6
- single: bfloat16 [256, 384], P(('groups', 'row')), parts along dimension 0, may hold values from -6 to 6
- token_mask: int32 [256], P('groups'), parts along dimension 0, may hold values 0 or 1
- chain_index: int32 [256], P('groups'), parts along dimension 0, may hold values from 0 to 7, as said below
- residue_index: int32 [256], P('groups'), parts along dimension 0, may hold values from 0 to 166, as said below
- pair_gain: float32 [128], replicated, may hold values from 0.25 to 1.75
- pair_norm_offset: float32 [128], replicated, may hold values from -3 to 3
- w_swish_a: bfloat16 [128, 512], replicated, may hold values from -0.5 to 0.5
- w_swish_b: bfloat16 [128, 512], replicated, may hold values from -0.5 to 0.5
- w_trans_out: bfloat16 [512, 128], replicated, may hold values from -0.25 to 0.25
- w_pair_bias: bfloat16 [128, 16], replicated, may hold values from -0.5 to 0.5
- w_project: bfloat16 [384, 1536], replicated, may hold values from -0.3125 to 0.3125
- w_out: bfloat16 [384, 384], replicated, may hold values from -0.3125 to 0.3125
- relative_position_bias: float32 [66, 16], replicated, may hold values from -6 to 300
Outputs:
- new_pair: bfloat16 [256, 128, 128], P(('groups', 'row')), parts along dimension 0
- single_update: bfloat16 [256, 384], P(('groups', 'row')), parts along dimension 0
The draws below stay inside these ranges and needn't reach their ends.
There are 2 independent parts, one for each index of `groups`. The reference program is written for one: setup_inputs(seed, part) draws one part's arguments, and reference() takes and returns one part's arrays. A program takes and returns all parts, laid end to end along the dimension named above; an argument that names none is the same for every part. Nothing has to cross between parts.
Inputs may be any that keep to these rules, and one draw needn't show every extreme that they name: `chain_index`: chain numbers never fall along the tokens, start at 0, and every chain 0 to 7 holds one token or more. `residue_index`: within a chain each token's residue number is one more than the previous token's.
All inputs are finite; a program needn't handle non-finite values.
Results may differ from the reference program's by a relative error of at most 0.014.
Values may be sent and summed in bfloat16 or wider, within the bound.
A program may use at most 64 MiB of HBM per device.

```python
import math
import jax
import jax.numpy as jnp
from jax import lax

C_PAIR = 128
FF = 512
HEADS = 16
HEAD_DIM = 24
D_SINGLE = 384
RELMAX = 32
BINS = 66
CHAINS = 8
TOKENS = 128


def chain_layout(key):
    cut_key = jax.random.fold_in(key, 11)
    shifted_key = jax.random.fold_in(key, 12)
    cuts = jax.random.permutation(cut_key, TOKENS - 1)[:CHAINS - 1] + 1
    starts = jnp.zeros((TOKENS,), jnp.int32).at[cuts].set(1)
    chain = jnp.cumsum(starts).astype(jnp.int32)
    position = jnp.arange(TOKENS, dtype=jnp.int32)
    first = lax.cummax(jnp.where(starts > 0, position, 0), axis=0)
    last_length = (TOKENS - first[TOKENS - 1]).astype(jnp.int32)
    shifts = jax.random.randint(shifted_key, (CHAINS,), 0, 40).astype(jnp.int32)
    shifts = shifts.at[0].set(0).at[CHAINS - 1].set(TOKENS + 39 - last_length)
    residue_number = (position - first + shifts[chain]).astype(jnp.int32)
    return (chain, residue_number)


def draw_chain_index(key, part):
    chain, residue_number = chain_layout(key)
    return chain


def draw_residue_index(key, part):
    chain, residue_number = chain_layout(key)
    return residue_number


def draw_relative_position_bias(key, part):
    base = jnp.clip(jax.random.normal(jax.random.fold_in(key, 21), (BINS, HEADS), jnp.float32), -6.0, 6.0)
    return base


def place_ends(result, stream_key, least, high):
    spot = [jax.random.randint(jax.random.fold_in(stream_key, axis), (), 0, length) for axis, length in enumerate(result.shape)]
    main_axis = result.shape.index(max(result.shape))
    neighbour = spot[:main_axis] + [(spot[main_axis] + 1) % result.shape[main_axis]] + spot[main_axis + 1:]
    return result.at[tuple(spot)].set(least).at[tuple(neighbour)].set(high)


def block_levels(own_key, extent, pieces, least, largest):
    factor_of, own = 1.0, jax.random.fold_in(own_key, 6)
    for dim, parts in pieces:
        heights = jnp.exp(jax.random.uniform(jax.random.fold_in(own, dim), (parts,), jnp.float32, least / len(pieces), largest / len(pieces)))
        factor_of = factor_of * jnp.repeat(heights, extent[dim] // parts).reshape([-1 if axis == dim else 1 for axis in range(len(extent))])
    return factor_of


def scatter_about(key, shape, scale, limit, pieces=(), held_as=jnp.bfloat16):
    drawn = scale * jax.random.normal(key, shape, jnp.float32)
    if pieces:
        drawn = drawn * block_levels(key, shape, pieces, -0.22, 0.18)
    return jnp.clip(drawn, -limit, limit).astype(held_as)


def setup_inputs(seed: int = 0, part: int = 0) -> dict:
    key_of = jax.random.split(jax.random.key(seed), 15)
    own_keys = jax.random.split(jax.random.fold_in(key_of[14], part), 15)
    pair = scatter_about(own_keys[0], (TOKENS, TOKENS, C_PAIR), 1.0, 6.0, ((0, 16),))
    single = scatter_about(own_keys[1], (TOKENS, D_SINGLE), 1.0, 6.0, ((0, 16),))
    token_mask = place_ends((jax.random.randint(own_keys[2], (TOKENS,), 0, 8) < 7).astype(jnp.int32), jax.random.fold_in(own_keys[2], 1), 0, 1)
    chain_index = draw_chain_index(jax.random.fold_in(jax.random.fold_in(key_of[14], part), 71), part)
    residue_index = draw_residue_index(jax.random.fold_in(jax.random.fold_in(key_of[14], part), 71), part)
    pair_gain = jnp.clip(1.0 + 0.15 * jax.random.normal(key_of[5], (C_PAIR,), jnp.float32), 0.25, 1.75)
    pair_norm_offset = scatter_about(key_of[6], (C_PAIR,), 0.5, 3.0, (), jnp.float32)
    w_swish_a = scatter_about(key_of[7], (C_PAIR, FF), C_PAIR ** -0.5, 0.5)
    w_swish_b = scatter_about(key_of[8], (C_PAIR, FF), C_PAIR ** -0.5, 0.5)
    w_trans_out = scatter_about(key_of[9], (FF, C_PAIR), FF ** -0.5, 0.25)
    w_pair_bias = scatter_about(key_of[10], (C_PAIR, HEADS), C_PAIR ** -0.5, 0.5)
    w_project = scatter_about(key_of[11], (D_SINGLE, 4 * D_SINGLE), D_SINGLE ** -0.5, 0.3125)
    w_out = scatter_about(key_of[12], (D_SINGLE, D_SINGLE), D_SINGLE ** -0.5, 0.3125)
    relative_position_bias = draw_relative_position_bias(jax.random.fold_in(key_of[14], 71), part)
    return dict(pair=pair, single=single, token_mask=token_mask, chain_index=chain_index, residue_index=residue_index, pair_gain=pair_gain, pair_norm_offset=pair_norm_offset, w_swish_a=w_swish_a, w_swish_b=w_swish_b, w_trans_out=w_trans_out, w_pair_bias=w_pair_bias, w_project=w_project, w_out=w_out, relative_position_bias=relative_position_bias)


epsilon = 1e-05

def layer_norm(value_rows):
    middle = lax.optimization_barrier(jnp.mean(value_rows, axis=-1, keepdims=True))
    centred = value_rows - middle
    spread = lax.optimization_barrier(jnp.mean(centred * centred, axis=-1, keepdims=True))
    return centred * lax.rsqrt(spread + epsilon)

def relative_bins(res_query, chain_query, res_key, chain_key):
    offset = jnp.clip(res_query[:, None] - res_key[None, :] + RELMAX, 0, 2 * RELMAX)
    return jnp.where(chain_query[:, None] == chain_key[None, :], offset, 2 * RELMAX + 1).astype(jnp.int32)

def transition_row(pair_row, pair_gain, pair_norm_offset, w_swish_a, w_swish_b, w_trans_out):
    normed = (layer_norm(pair_row.astype(jnp.float32)) * pair_gain + pair_norm_offset).astype(jnp.bfloat16)
    first = jnp.dot(normed, w_swish_a, preferred_element_type=jnp.float32)
    second_operand = jnp.dot(normed, w_swish_b, preferred_element_type=jnp.float32)
    hidden = (jax.nn.silu(first) * second_operand).astype(jnp.bfloat16)
    updated = (pair_row.astype(jnp.float32) + jnp.dot(hidden, w_trans_out, preferred_element_type=jnp.float32)).astype(jnp.bfloat16)
    bias_input = layer_norm(updated.astype(jnp.float32)).astype(jnp.bfloat16)
    return (updated, bias_input)

def reference(pair, single, token_mask, chain_index, residue_index, pair_gain, pair_norm_offset, w_swish_a, w_swish_b, w_trans_out, w_pair_bias, w_project, w_out, relative_position_bias):

    def one_row(pair_row):
        updated, bias_input = transition_row(pair_row, pair_gain, pair_norm_offset, w_swish_a, w_swish_b, w_trans_out)
        bias_row = jnp.dot(bias_input, w_pair_bias, preferred_element_type=jnp.float32).astype(jnp.bfloat16)
        return (updated, bias_row)
    new_pair, bias_rows = lax.map(one_row, pair)
    width = HEADS * HEAD_DIM
    normed = layer_norm(single.astype(jnp.float32)).astype(jnp.bfloat16)
    projected = jnp.dot(normed, w_project, preferred_element_type=jnp.float32).astype(jnp.bfloat16)
    queries = projected[:, :width].reshape(TOKENS, HEADS, HEAD_DIM).astype(jnp.float32)
    keys_all = projected[:, width:2 * width].reshape(TOKENS, HEADS, HEAD_DIM).astype(jnp.float32)
    values_all = projected[:, 2 * width:3 * width].reshape(TOKENS, HEADS, HEAD_DIM).astype(jnp.float32)
    gates = projected[:, 3 * width:].astype(jnp.float32)
    scores = jnp.einsum('ihd,jhd->hij', queries, keys_all) / math.sqrt(HEAD_DIM)
    bins = relative_bins(residue_index, chain_index, residue_index, chain_index)
    scores = scores + jnp.transpose(bias_rows.astype(jnp.float32), (2, 0, 1)) + jnp.transpose(relative_position_bias[bins], (2, 0, 1))
    scores = jnp.where(token_mask[None, None, :] > 0, scores, -1000000000.0)
    highest = lax.optimization_barrier(jnp.max(scores, axis=-1, keepdims=True))
    expons = jnp.exp(scores - highest)
    totals = lax.optimization_barrier(jnp.sum(expons, axis=-1))
    weights = lax.optimization_barrier(expons.astype(jnp.bfloat16)).astype(jnp.float32)
    attended_rows = jnp.einsum('hij,jhd->ihd', weights, values_all) / jnp.transpose(totals)[:, :, None]
    gated = (jax.nn.sigmoid(gates) * attended_rows.reshape(TOKENS, width)).astype(jnp.bfloat16)
    single_update = jnp.dot(gated, w_out, preferred_element_type=jnp.float32).astype(jnp.bfloat16)
    return (new_pair, single_update)
```

```python
import functools
import math

import jax
import jax.numpy as jnp
from jax import lax
from jax.experimental import pallas as pl
from jax.experimental.pallas import tpu as pltpu
from jax.sharding import PartitionSpec as P

HEADS = 16
HEAD_DIM = 24
RELMAX = 32
BINS = 66
CLASSES = 80
ROWS_AT_ONCE = 512
LANES = 128
GRANT = 24 * 1024 * 1024

epsilon = 1e-05
F32 = jnp.float32
BF16 = jnp.bfloat16


def layer_norm(value_rows):
    middle = jnp.mean(value_rows, axis=-1, keepdims=True)
    centred = value_rows - middle
    spread = jnp.mean(centred * centred, axis=-1, keepdims=True)
    return centred * lax.rsqrt(spread + epsilon)


def dot(a, b):
    return jnp.dot(a, b, preferred_element_type=F32)


def dot_nt(a, b):
    return lax.dot_general(a, b, (((1,), (1,)), ((), ())), preferred_element_type=F32)


def other(me, step, devices):
    return step + (step - me + devices) // devices


def own_columns(local, width):
    place = lax.broadcasted_iota(jnp.int32, (HEADS, local, width), 2) - HEAD_DIM * (
        lax.broadcasted_iota(jnp.int32, (HEADS, local, width), 0)
    )
    return (place >= 0) & (place < HEAD_DIM)


def kernel(
    devices,
    pair_hbm,
    single_hbm,
    chain_hbm,
    res_hbm,
    gain_hbm,
    offset_hbm,
    wa_hbm,
    wb_hbm,
    wt_hbm,
    wpb_hbm,
    wp_hbm,
    table_hbm,
    new_pair_ref,
    bias_ref,
    keys_ref,
    spread_ref,
    gates_ref,
    wv_ref,
    pair,
    gathered,
    bias,
    chain,
    res,
    gain,
    offset,
    wa,
    wb,
    wt,
    wpb,
    wp,
    table,
    load_sem,
    send_sem,
    recv_sem,
):
    me = lax.axis_index("row")
    local, tokens, channels = pair.shape
    width = gathered.shape[2]

    loads = [
        pltpu.make_async_copy(src, dst, load_sem.at[i])
        for i, (src, dst) in enumerate(
            (
                (single_hbm, gathered.at[me]),
                (chain_hbm, chain),
                (res_hbm, res),
                (table_hbm, table),
                (pair_hbm, pair),
                (gain_hbm, gain),
                (offset_hbm, offset),
                (wa_hbm, wa),
                (wb_hbm, wb),
                (wt_hbm, wt),
                (wpb_hbm, wpb),
                (wp_hbm, wp),
            )
        )
    ]
    barrier = pltpu.get_barrier_semaphore()

    def greet(step, carry):
        pl.semaphore_signal(
            barrier,
            inc=1,
            device_id={"row": other(me, step, devices)},
            device_id_type=pl.DeviceIdType.MESH,
        )
        return carry

    for load in loads[:1]:
        load.start()
    lax.fori_loop(0, devices - 1, greet, 0, unroll=devices <= 16)
    for load in loads[1:]:
        load.start()

    def copy_between(sender, receiver):
        return pltpu.make_async_remote_copy(
            src_ref=gathered.at[sender],
            dst_ref=gathered.at[sender],
            send_sem=send_sem,
            recv_sem=recv_sem,
            device_id={"row": receiver},
            device_id_type=pl.DeviceIdType.MESH,
        )

    loads[0].wait()
    at_once = max(1, ROWS_AT_ONCE // tokens)
    span = min(tokens, ROWS_AT_ONCE)
    pieces = tokens // span

    def transition(chunk, half_wa, wpb_t):
        row = pl.ds((chunk // pieces) * at_once, at_once)
        start = (chunk % pieces) * span
        if not isinstance(start, int):
            start = pl.multiple_of(start, span)
        col = pl.ds(start, span)
        x = pair[row, col, :].reshape(at_once * span, channels).astype(F32)
        normed = (layer_norm(x) * gain[...] + offset[...]).astype(BF16)
        h = dot(normed, half_wa)
        second = dot(normed, wb[...])
        hidden = ((h + h * jnp.tanh(h)) * second).astype(BF16)
        updated = (x + dot(hidden, wt[...])).astype(BF16)
        new_pair_ref[row, col, :] = updated.reshape(at_once, span, channels)
        bias_input = layer_norm(updated.astype(F32)).astype(BF16)
        head_rows = dot_nt(wpb_t, bias_input).astype(BF16).astype(F32)
        for i in range(at_once):
            at = ((chunk // pieces) * at_once + i, slice(None), col)
            bias[at] = bias[at] + head_rows[:, i * span : (i + 1) * span]

    chunks = (local // at_once) * pieces
    def pair_work():
        for load in loads[1:4]:
            load.wait()
        at = lax.broadcasted_iota(jnp.int32, (local, tokens), 1)
        own_at = lax.broadcasted_iota(jnp.int32, (local, tokens), 0) + me * local
        res_all = res[...].astype(F32)
        chain_all = chain[...].astype(F32)
        here = at == own_at
        own_res = jnp.sum(jnp.where(here, res_all, 0.0), axis=1, keepdims=True)
        own_chain = jnp.sum(jnp.where(here, chain_all, 0.0), axis=1, keepdims=True)
        bins = jnp.where(
            own_chain == chain_all,
            jnp.clip(own_res - res_all + RELMAX, 0.0, 2.0 * RELMAX),
            2.0 * RELMAX + 1.0,
        ).astype(jnp.int32)
        table_t = jnp.concatenate(
            [table[...], jnp.zeros((HEADS, CLASSES - BINS), F32)], axis=1
        )
        high = table_t.astype(BF16)
        rest = table_t - high.astype(F32)
        middle = rest.astype(BF16)
        low = (rest - middle.astype(F32)).astype(BF16)
        classes = lax.broadcasted_iota(jnp.int32, (CLASSES, tokens), 0)
        for r in range(local):
            hot = jnp.where(classes == bins[r : r + 1, :], 1.0, 0.0).astype(BF16)
            bias[r] = dot(high, hot) + (dot(middle, hot) + dot(low, hot))

        for load in loads[4:11]:
            load.wait()
        half_wa = wa[...] * BF16(0.5)
        wpb_t = wpb[...]

        if chunks <= 8:
            for chunk in range(chunks):
                transition(chunk, half_wa, wpb_t)
        else:

            def body(chunk, carry):
                transition(chunk, half_wa, wpb_t)
                return carry

            lax.fori_loop(0, chunks, body, 0)

    ahead = me < 2
    pl.when(ahead)(pair_work)
    pl.semaphore_wait(barrier, devices - 1)

    def send(step, carry):
        copy_between(me, other(me, step, devices)).start()
        return carry

    lax.fori_loop(0, devices - 1, send, 0, unroll=devices <= 16)
    pl.when(jnp.logical_not(ahead))(pair_work)

    loads[11].wait()
    own = layer_norm(gathered[me].astype(F32)).astype(BF16)
    queries = dot(own, wp[:, :width]).astype(BF16).astype(F32)
    gates = dot(own, wp[:, 3 * width :]).astype(BF16).astype(F32)
    gates_ref[...] = jax.nn.sigmoid(gates)
    wv_ref[...] = wp[:, 2 * width : 3 * width]
    mine = own_columns(local, width)
    spread_queries = jnp.where(mine, queries[None, :, :], 0.0)
    spread_queries = spread_queries.reshape(HEADS * local, width).astype(BF16)
    spread_queries = dot_nt(spread_queries, wp[:, width : 2 * width]) * (
        1.0 / math.sqrt(HEAD_DIM)
    )
    spread_ref[...] = spread_queries.astype(BF16)
    for i in range(local):
        bias_ref[:, i, :] = bias[i]

    partners = gathered.at[pl.ds(0, devices - 1)]
    everyone = pltpu.make_async_remote_copy(
        src_ref=partners,
        dst_ref=partners,
        send_sem=send_sem,
        recv_sem=recv_sem,
        device_id={"row": other(me, 0, devices)},
        device_id_type=pl.DeviceIdType.MESH,
    )
    everyone.wait_send()
    everyone.wait_recv()
    normed = layer_norm(gathered[...].astype(F32).reshape(tokens, width)).astype(BF16)
    keys_ref[...] = normed


def attention(
    new_pair_from,
    bias,
    keys,
    spread_queries,
    gates,
    wv,
    mask,
    wo,
    new_pair_ref,
    update_ref,
    update,
    out_sem,
    update_sem,
):
    local, width = gates.shape
    tokens = keys.shape[0]
    out = pltpu.make_async_copy(new_pair_from, new_pair_ref, out_sem)
    out.start()
    scores = dot_nt(spread_queries[...], keys[...])
    scores = scores + bias[...].reshape(HEADS * local, tokens)
    scores = jnp.where(mask[...] > 0, scores, -1000000000.0)
    expons = jnp.exp(scores - jnp.max(scores, axis=1, keepdims=True)).astype(BF16)
    values = dot(keys[...], wv[...]).astype(BF16)
    values = jnp.concatenate([values, jnp.ones((tokens, LANES), BF16)], axis=1)
    spread = dot(expons, values)
    shares = 1.0 / spread[:, width:]
    column = lax.broadcasted_iota(jnp.int32, (local, LANES), 1)
    pieces = []
    for first in range(0, width, LANES):
        piece = jnp.zeros((local, LANES), F32)
        for head in range(HEADS):
            begin, end = head * HEAD_DIM - first, (head + 1) * HEAD_DIM - first
            if begin < LANES and end > 0:
                rows = slice(head * local, (head + 1) * local)
                part = spread[rows, first : first + LANES] * shares[rows]
                piece = jnp.where((column >= begin) & (column < end), part, piece)
        pieces.append(piece)
    attended = jnp.concatenate(pieces, axis=1)
    gated = (gates[...] * attended).astype(BF16)
    update[...] = dot(gated, wo[...]).astype(BF16)
    done = pltpu.make_async_copy(update, update_ref, update_sem)
    done.start()
    done.wait()
    pltpu.make_async_copy(new_pair_from, new_pair_ref, out_sem).wait()


def on_device(
    devices,
    pair,
    single,
    token_mask,
    chain_index,
    residue_index,
    pair_gain,
    pair_norm_offset,
    w_swish_a,
    w_swish_b,
    w_trans_out,
    w_pair_bias,
    w_project,
    w_out,
    relative_position_bias,
):
    def line(vector):
        return vector.reshape(1, vector.shape[0])

    operands = (
        pair,
        single,
        line(chain_index),
        line(residue_index),
        line(pair_gain),
        line(pair_norm_offset),
        w_swish_a,
        w_swish_b,
        w_trans_out,
        w_pair_bias.T,
        w_project,
        relative_position_bias.T,
    )
    local, tokens, _ = pair.shape
    width = single.shape[1]
    anywhere = pl.BlockSpec(memory_space=pl.ANY)
    vmem = pl.BlockSpec(memory_space=pltpu.VMEM)
    held = [
        pltpu.VMEM(pair.shape, pair.dtype),
        pltpu.VMEM((devices,) + single.shape, single.dtype),
        pltpu.VMEM((local, HEADS, tokens), F32),
    ]
    held += [pltpu.VMEM(x.shape, x.dtype) for x in operands[2:]]
    operands = [pltpu.with_memory_space_constraint(x, pltpu.HBM) for x in operands]
    handed = pl.pallas_call(
        functools.partial(kernel, devices),
        out_shape=(
            jax.ShapeDtypeStruct(pair.shape, BF16),
            jax.ShapeDtypeStruct((HEADS, local, tokens), F32),
            jax.ShapeDtypeStruct((tokens, width), BF16),
            jax.ShapeDtypeStruct((local * HEADS, width), BF16),
            jax.ShapeDtypeStruct((local, width), F32),
            jax.ShapeDtypeStruct((width, width), BF16),
        ),
        in_specs=[anywhere] * len(operands),
        out_specs=(vmem,) * 6,
        scratch_shapes=held
        + [
            pltpu.SemaphoreType.DMA((len(operands),)),
            pltpu.SemaphoreType.DMA,
            pltpu.SemaphoreType.DMA,
        ],
        compiler_params=pltpu.CompilerParams(
            collective_id=0, has_side_effects=True, vmem_limit_bytes=GRANT
        ),
        name="pair_tail",
    )(*operands)
    return pl.pallas_call(
        attention,
        out_shape=(
            jax.ShapeDtypeStruct(pair.shape, BF16),
            jax.ShapeDtypeStruct(single.shape, BF16),
        ),
        in_specs=[anywhere] + [vmem] * 7,
        out_specs=(anywhere, anywhere),
        scratch_shapes=[pltpu.VMEM(single.shape, BF16), pltpu.SemaphoreType.DMA, pltpu.SemaphoreType.DMA],
        compiler_params=pltpu.CompilerParams(vmem_limit_bytes=GRANT),
        name="single_attention",
    )(*handed, line(token_mask), w_out)


def solution(mesh):
    rows = P(("groups", "row"))
    return jax.shard_map(
        functools.partial(on_device, mesh.shape["row"]),
        mesh=mesh,
        in_specs=(rows, rows) + (P("groups"),) * 3 + (P(),) * 9,
        out_specs=(rows, rows),
        check_vma=False,
    )
```

```python
import functools
import math

import jax
import jax.numpy as jnp
from jax import lax
from jax.experimental import pallas as pl
from jax.experimental.pallas import tpu as pltpu
from jax.sharding import PartitionSpec as P

HEADS = 16
HEAD_DIM = 24
RELMAX = 32
BINS = 66
CLASSES = 80
ROWS_AT_ONCE = 512
LANES = 128
FRINGE = 2
GRANT = 24 * 1024 * 1024

epsilon = 1e-05
F32 = jnp.float32
BF16 = jnp.bfloat16


def layer_norm(value_rows):
    middle = jnp.mean(value_rows, axis=-1, keepdims=True)
    centred = value_rows - middle
    spread = jnp.mean(centred * centred, axis=-1, keepdims=True)
    return centred * lax.rsqrt(spread + epsilon)


def dot(a, b):
    return jnp.dot(a, b, preferred_element_type=F32)


def dot_nt(a, b):
    return lax.dot_general(a, b, (((1,), (1,)), ((), ())), preferred_element_type=F32)


def other(me, step, devices):
    return step + (step - me + devices) // devices


def own_columns(local, width):
    place = lax.broadcasted_iota(jnp.int32, (HEADS, local, width), 2) - HEAD_DIM * (
        lax.broadcasted_iota(jnp.int32, (HEADS, local, width), 0)
    )
    return (place >= 0) & (place < HEAD_DIM)


def kernel(
    devices,
    pair_hbm,
    single_hbm,
    chain_hbm,
    res_hbm,
    gain_hbm,
    offset_hbm,
    wa_hbm,
    wb_hbm,
    wt_hbm,
    wpb_hbm,
    wp_hbm,
    table_hbm,
    new_pair_ref,
    bias_ref,
    keys_ref,
    spread_ref,
    gates_ref,
    wv_ref,
    pair,
    gathered,
    bias,
    chain,
    res,
    gain,
    offset,
    wa,
    wb,
    wt,
    wpb,
    wp,
    table,
    load_sem,
    send_sem,
    recv_sem,
    late_sem,
):
    me = lax.axis_index("row")
    local, tokens, channels = pair.shape
    width = gathered.shape[2]

    loads = [
        pltpu.make_async_copy(src, dst, load_sem.at[i])
        for i, (src, dst) in enumerate(
            (
                (single_hbm, gathered.at[me]),
                (chain_hbm, chain),
                (res_hbm, res),
                (table_hbm, table),
                (pair_hbm, pair),
                (gain_hbm, gain),
                (offset_hbm, offset),
                (wa_hbm, wa),
                (wb_hbm, wb),
                (wt_hbm, wt),
                (wpb_hbm, wpb),
                (wp_hbm, wp),
            )
        )
    ]
    barrier = pltpu.get_barrier_semaphore()

    last = devices - FRINGE
    is_early, is_late = me < FRINGE, me >= last
    is_middle = jnp.logical_not(jnp.logical_or(is_early, is_late))

    def repeat(count, act):
        def body(step, carry):
            act(step)
            return carry

        lax.fori_loop(0, count, body, 0, unroll=devices <= 16)

    def greet(receiver):
        pl.semaphore_signal(
            barrier,
            inc=1,
            device_id={"row": receiver},
            device_id_type=pl.DeviceIdType.MESH,
        )

    def send(receiver, arrival):
        pltpu.make_async_remote_copy(
            src_ref=gathered.at[me],
            dst_ref=gathered.at[me],
            send_sem=send_sem,
            recv_sem=arrival,
            device_id={"row": receiver},
            device_id_type=pl.DeviceIdType.MESH,
        ).start()

    def blocks(count, arrival):
        some = gathered.at[pl.ds(0, count)]
        return pltpu.make_async_remote_copy(
            src_ref=some,
            dst_ref=some,
            send_sem=send_sem,
            recv_sem=arrival,
            device_id={"row": other(me, 0, devices)},
            device_id_type=pl.DeviceIdType.MESH,
        )

    loads[0].start()

    @pl.when(is_late)
    def _():
        for receiver in range(FRINGE):
            greet(receiver)
        repeat(FRINGE - 1, lambda step: greet(last + other(me - last, step, FRINGE)))

    @pl.when(jnp.logical_not(is_late))
    def _():
        repeat(devices - 1, lambda step: greet(other(me, step, devices)))

    for load in loads[1:]:
        load.start()

    loads[0].wait()
    at_once = max(1, ROWS_AT_ONCE // tokens)
    span = min(tokens, ROWS_AT_ONCE)
    pieces = tokens // span

    def transition(chunk, half_wa, wpb_t):
        row = pl.ds((chunk // pieces) * at_once, at_once)
        start = (chunk % pieces) * span
        if not isinstance(start, int):
            start = pl.multiple_of(start, span)
        col = pl.ds(start, span)
        x = pair[row, col, :].reshape(at_once * span, channels).astype(F32)
        normed = (layer_norm(x) * gain[...] + offset[...]).astype(BF16)
        h = dot(normed, half_wa)
        second = dot(normed, wb[...])
        hidden = ((h + h * jnp.tanh(h)) * second).astype(BF16)
        updated = (x + dot(hidden, wt[...])).astype(BF16)
        new_pair_ref[row, col, :] = updated.reshape(at_once, span, channels)
        bias_input = layer_norm(updated.astype(F32)).astype(BF16)
        head_rows = dot_nt(wpb_t, bias_input).astype(BF16).astype(F32)
        for i in range(at_once):
            at = ((chunk // pieces) * at_once + i, slice(None), col)
            bias[at] = bias[at] + head_rows[:, i * span : (i + 1) * span]

    chunks = (local // at_once) * pieces
    def answer():
        @pl.when(is_middle)
        def _():
            blocks(FRINGE, late_sem).wait_recv()
            repeat(FRINGE, lambda step: send(last + step, recv_sem))

    def pair_work(answer=lambda: None):
        for load in loads[1:4]:
            load.wait()
        at = lax.broadcasted_iota(jnp.int32, (local, tokens), 1)
        own_at = lax.broadcasted_iota(jnp.int32, (local, tokens), 0) + me * local
        res_all = res[...].astype(F32)
        chain_all = chain[...].astype(F32)
        here = at == own_at
        own_res = jnp.sum(jnp.where(here, res_all, 0.0), axis=1, keepdims=True)
        own_chain = jnp.sum(jnp.where(here, chain_all, 0.0), axis=1, keepdims=True)
        bins = jnp.where(
            own_chain == chain_all,
            jnp.clip(own_res - res_all + RELMAX, 0.0, 2.0 * RELMAX),
            2.0 * RELMAX + 1.0,
        ).astype(jnp.int32)
        table_t = jnp.concatenate(
            [table[...], jnp.zeros((HEADS, CLASSES - BINS), F32)], axis=1
        )
        high = table_t.astype(BF16)
        rest = table_t - high.astype(F32)
        middle = rest.astype(BF16)
        low = (rest - middle.astype(F32)).astype(BF16)
        classes = lax.broadcasted_iota(jnp.int32, (CLASSES, tokens), 0)
        for r in range(local):
            hot = jnp.where(classes == bins[r : r + 1, :], 1.0, 0.0).astype(BF16)
            bias[r] = dot(high, hot) + (dot(middle, hot) + dot(low, hot))

        for load in loads[4:11]:
            load.wait()
        half_wa = wa[...] * BF16(0.5)
        wpb_t = wpb[...]

        if chunks <= 8:
            for chunk in range(chunks):
                if chunk == chunks - 1:
                    answer()
                transition(chunk, half_wa, wpb_t)
        else:

            def body(chunk, carry):
                transition(chunk, half_wa, wpb_t)
                return carry

            lax.fori_loop(0, chunks, body, 0)
            answer()

    pl.when(is_early)(pair_work)

    @pl.when(is_late)
    def _():
        pl.semaphore_wait(barrier, devices - 1)
        for receiver in range(FRINGE):
            send(receiver, late_sem)
        repeat(FRINGE - 1, lambda step: send(last + other(me - last, step, FRINGE), late_sem))
        repeat(last - FRINGE, lambda step: send(FRINGE + step, late_sem))

    @pl.when(is_middle)
    def _():
        pl.semaphore_wait(barrier, last - 1)
        repeat(last - 1, lambda step: send(other(me, step, devices), recv_sem))

    @pl.when(is_early)
    def _():
        pl.semaphore_wait(barrier, devices - 1)
        repeat(FRINGE, lambda step: send(last + step, recv_sem))
        repeat(last - 1, lambda step: send(other(me, step, devices), recv_sem))

    pl.when(jnp.logical_not(is_early))(lambda: pair_work(answer))

    loads[11].wait()
    own = layer_norm(gathered[me].astype(F32)).astype(BF16)
    queries = dot(own, wp[:, :width]).astype(BF16).astype(F32)
    gates = dot(own, wp[:, 3 * width :]).astype(BF16).astype(F32)
    gates_ref[...] = jax.nn.sigmoid(gates)
    wv_ref[...] = wp[:, 2 * width : 3 * width]
    mine = own_columns(local, width)
    spread_queries = jnp.where(mine, queries[None, :, :], 0.0)
    spread_queries = spread_queries.reshape(HEADS * local, width).astype(BF16)
    spread_queries = dot_nt(spread_queries, wp[:, width : 2 * width]) * (
        1.0 / math.sqrt(HEAD_DIM)
    )
    spread_ref[...] = spread_queries.astype(BF16)
    for i in range(local):
        bias_ref[:, i, :] = bias[i]

    @pl.when(is_middle)
    def _():
        blocks(last - 1, recv_sem).wait_recv()

    @pl.when(is_late)
    def _():
        blocks(FRINGE - 1, late_sem).wait_recv()
        blocks(last, recv_sem).wait_recv()

    @pl.when(is_early)
    def _():
        blocks(last - 1, recv_sem).wait_recv()
        blocks(FRINGE, late_sem).wait_recv()

    blocks(devices - 1, recv_sem).wait_send()
    normed = layer_norm(gathered[...].astype(F32).reshape(tokens, width)).astype(BF16)
    keys_ref[...] = normed


def attention(
    new_pair_from,
    bias,
    keys,
    spread_queries,
    gates,
    wv,
    mask,
    wo,
    new_pair_ref,
    update_ref,
    update,
    out_sem,
    update_sem,
):
    local, width = gates.shape
    tokens = keys.shape[0]
    out = pltpu.make_async_copy(new_pair_from, new_pair_ref, out_sem)
    out.start()
    scores = dot_nt(spread_queries[...], keys[...])
    scores = scores + bias[...].reshape(HEADS * local, tokens)
    scores = jnp.where(mask[...] > 0, scores, -1000000000.0)
    expons = jnp.exp(scores - jnp.max(scores, axis=1, keepdims=True)).astype(BF16)
    values = dot(keys[...], wv[...]).astype(BF16)
    values = jnp.concatenate([values, jnp.ones((tokens, LANES), BF16)], axis=1)
    spread = dot(expons, values)
    shares = 1.0 / spread[:, width:]
    column = lax.broadcasted_iota(jnp.int32, (local, LANES), 1)
    pieces = []
    for first in range(0, width, LANES):
        piece = jnp.zeros((local, LANES), F32)
        for head in range(HEADS):
            begin, end = head * HEAD_DIM - first, (head + 1) * HEAD_DIM - first
            if begin < LANES and end > 0:
                rows = slice(head * local, (head + 1) * local)
                part = spread[rows, first : first + LANES] * shares[rows]
                piece = jnp.where((column >= begin) & (column < end), part, piece)
        pieces.append(piece)
    attended = jnp.concatenate(pieces, axis=1)
    gated = (gates[...] * attended).astype(BF16)
    update[...] = dot(gated, wo[...]).astype(BF16)
    done = pltpu.make_async_copy(update, update_ref, update_sem)
    done.start()
    done.wait()
    pltpu.make_async_copy(new_pair_from, new_pair_ref, out_sem).wait()


def on_device(
    devices,
    pair,
    single,
    token_mask,
    chain_index,
    residue_index,
    pair_gain,
    pair_norm_offset,
    w_swish_a,
    w_swish_b,
    w_trans_out,
    w_pair_bias,
    w_project,
    w_out,
    relative_position_bias,
):
    def line(vector):
        return vector.reshape(1, vector.shape[0])

    operands = (
        pair,
        single,
        line(chain_index),
        line(residue_index),
        line(pair_gain),
        line(pair_norm_offset),
        w_swish_a,
        w_swish_b,
        w_trans_out,
        w_pair_bias.T,
        w_project,
        relative_position_bias.T,
    )
    local, tokens, _ = pair.shape
    width = single.shape[1]
    anywhere = pl.BlockSpec(memory_space=pl.ANY)
    vmem = pl.BlockSpec(memory_space=pltpu.VMEM)
    held = [
        pltpu.VMEM(pair.shape, pair.dtype),
        pltpu.VMEM((devices,) + single.shape, single.dtype),
        pltpu.VMEM((local, HEADS, tokens), F32),
    ]
    held += [pltpu.VMEM(x.shape, x.dtype) for x in operands[2:]]
    operands = [pltpu.with_memory_space_constraint(x, pltpu.HBM) for x in operands]
    handed = pl.pallas_call(
        functools.partial(kernel, devices),
        out_shape=(
            jax.ShapeDtypeStruct(pair.shape, BF16),
            jax.ShapeDtypeStruct((HEADS, local, tokens), F32),
            jax.ShapeDtypeStruct((tokens, width), BF16),
            jax.ShapeDtypeStruct((local * HEADS, width), BF16),
            jax.ShapeDtypeStruct((local, width), F32),
            jax.ShapeDtypeStruct((width, width), BF16),
        ),
        in_specs=[anywhere] * len(operands),
        out_specs=(vmem,) * 6,
        scratch_shapes=held
        + [
            pltpu.SemaphoreType.DMA((len(operands),)),
            pltpu.SemaphoreType.DMA,
            pltpu.SemaphoreType.DMA,
            pltpu.SemaphoreType.DMA,
        ],
        compiler_params=pltpu.CompilerParams(
            collective_id=0, has_side_effects=True, vmem_limit_bytes=GRANT
        ),
        name="pair_tail",
    )(*operands)
    return pl.pallas_call(
        attention,
        out_shape=(
            jax.ShapeDtypeStruct(pair.shape, BF16),
            jax.ShapeDtypeStruct(single.shape, BF16),
        ),
        in_specs=[anywhere] + [vmem] * 7,
        out_specs=(anywhere, anywhere),
        scratch_shapes=[pltpu.VMEM(single.shape, BF16), pltpu.SemaphoreType.DMA, pltpu.SemaphoreType.DMA],
        compiler_params=pltpu.CompilerParams(vmem_limit_bytes=GRANT),
        name="single_attention",
    )(*handed, line(token_mask), w_out)


def solution(mesh):
    rows = P(("groups", "row"))
    return jax.shard_map(
        functools.partial(on_device, mesh.shape["row"]),
        mesh=mesh,
        in_specs=(rows, rows) + (P("groups"),) * 3 + (P(),) * 9,
        out_specs=(rows, rows),
        check_vma=False,
    )
```

```python
import functools
import math

import jax
import jax.numpy as jnp
from jax import lax
from jax.experimental import pallas as pl
from jax.experimental.pallas import tpu as pltpu
from jax.sharding import PartitionSpec as P

HEADS = 16
HEAD_DIM = 24
RELMAX = 32
BINS = 66
CLASSES = 80
ROWS_AT_ONCE = 512
LANES = 128
FRINGE = 2
GRANT = 24 * 1024 * 1024

epsilon = 1e-05
F32 = jnp.float32
BF16 = jnp.bfloat16


def layer_norm(value_rows):
    middle = jnp.mean(value_rows, axis=-1, keepdims=True)
    centred = value_rows - middle
    spread = jnp.mean(centred * centred, axis=-1, keepdims=True)
    return centred * lax.rsqrt(spread + epsilon)


def dot(a, b):
    return jnp.dot(a, b, preferred_element_type=F32)


def dot_nt(a, b):
    return lax.dot_general(a, b, (((1,), (1,)), ((), ())), preferred_element_type=F32)


def other(me, step, devices):
    return step + (step - me + devices) // devices


def own_columns(local, width):
    place = lax.broadcasted_iota(jnp.int32, (HEADS, local, width), 2) - HEAD_DIM * (
        lax.broadcasted_iota(jnp.int32, (HEADS, local, width), 0)
    )
    return (place >= 0) & (place < HEAD_DIM)


def kernel(
    devices,
    pair_hbm,
    single_hbm,
    chain_hbm,
    res_hbm,
    gain_hbm,
    offset_hbm,
    wa_hbm,
    wb_hbm,
    wt_hbm,
    wpb_hbm,
    wp_hbm,
    table_hbm,
    new_pair_ref,
    bias_ref,
    keys_ref,
    spread_ref,
    gates_ref,
    wv_ref,
    pair,
    single,
    bias,
    chain,
    res,
    gain,
    offset,
    wa,
    wb,
    wt,
    wpb,
    wp,
    table,
    load_sem,
    send_sem,
    recv_sem,
    late_sem,
):
    me = lax.axis_index("row")
    local, tokens, channels = pair.shape
    width = single.shape[1]
    mine_at = pl.ds(pl.multiple_of(me * local, local), local)

    loads = [
        pltpu.make_async_copy(src, dst, load_sem.at[i])
        for i, (src, dst) in enumerate(
            (
                (single_hbm, single),
                (chain_hbm, chain),
                (res_hbm, res),
                (table_hbm, table),
                (pair_hbm, pair),
                (gain_hbm, gain),
                (offset_hbm, offset),
                (wa_hbm, wa),
                (wb_hbm, wb),
                (wt_hbm, wt),
                (wpb_hbm, wpb),
                (wp_hbm, wp),
            )
        )
    ]
    barrier = pltpu.get_barrier_semaphore()

    last = devices - FRINGE
    is_early, is_late = me < FRINGE, me >= last
    is_middle = jnp.logical_not(jnp.logical_or(is_early, is_late))

    def repeat(count, act):
        def body(step, carry):
            act(step)
            return carry

        lax.fori_loop(0, count, body, 0, unroll=devices <= 16)

    def greet(receiver):
        pl.semaphore_signal(
            barrier,
            inc=1,
            device_id={"row": receiver},
            device_id_type=pl.DeviceIdType.MESH,
        )

    def send(receiver, arrival):
        pltpu.make_async_remote_copy(
            src_ref=keys_ref.at[mine_at],
            dst_ref=keys_ref.at[mine_at],
            send_sem=send_sem,
            recv_sem=arrival,
            device_id={"row": receiver},
            device_id_type=pl.DeviceIdType.MESH,
        ).start()

    def blocks(count, arrival):
        some = keys_ref.at[pl.ds(0, count * local)]
        return pltpu.make_async_remote_copy(
            src_ref=some,
            dst_ref=some,
            send_sem=send_sem,
            recv_sem=arrival,
            device_id={"row": other(me, 0, devices)},
            device_id_type=pl.DeviceIdType.MESH,
        )

    loads[0].start()

    @pl.when(is_late)
    def _():
        for receiver in range(FRINGE):
            greet(receiver)
        repeat(FRINGE - 1, lambda step: greet(last + other(me - last, step, FRINGE)))

    @pl.when(jnp.logical_not(is_late))
    def _():
        repeat(devices - 1, lambda step: greet(other(me, step, devices)))

    for load in loads[1:]:
        load.start()

    loads[0].wait()
    keys_ref[mine_at, :] = layer_norm(single[...].astype(F32)).astype(BF16)
    at_once = max(1, ROWS_AT_ONCE // tokens)
    span = min(tokens, ROWS_AT_ONCE)
    pieces = tokens // span

    def transition(chunk, half_wa, wpb_t):
        row = pl.ds((chunk // pieces) * at_once, at_once)
        start = (chunk % pieces) * span
        if not isinstance(start, int):
            start = pl.multiple_of(start, span)
        col = pl.ds(start, span)
        x = pair[row, col, :].reshape(at_once * span, channels).astype(F32)
        normed = (layer_norm(x) * gain[...] + offset[...]).astype(BF16)
        h = dot(normed, half_wa)
        second = dot(normed, wb[...])
        hidden = ((h + h * jnp.tanh(h)) * second).astype(BF16)
        updated = (x + dot(hidden, wt[...])).astype(BF16)
        new_pair_ref[row, col, :] = updated.reshape(at_once, span, channels)
        bias_input = layer_norm(updated.astype(F32)).astype(BF16)
        head_rows = dot_nt(wpb_t, bias_input).astype(BF16).astype(F32)
        for i in range(at_once):
            at = ((chunk // pieces) * at_once + i, slice(None), col)
            bias[at] = bias[at] + head_rows[:, i * span : (i + 1) * span]

    chunks = (local // at_once) * pieces
    def answer():
        @pl.when(is_middle)
        def _():
            blocks(FRINGE, late_sem).wait_recv()
            repeat(FRINGE, lambda step: send(last + step, recv_sem))

    def pair_work(answer=lambda: None):
        for load in loads[1:4]:
            load.wait()
        at = lax.broadcasted_iota(jnp.int32, (local, tokens), 1)
        own_at = lax.broadcasted_iota(jnp.int32, (local, tokens), 0) + me * local
        res_all = res[...].astype(F32)
        chain_all = chain[...].astype(F32)
        here = at == own_at
        own_res = jnp.sum(jnp.where(here, res_all, 0.0), axis=1, keepdims=True)
        own_chain = jnp.sum(jnp.where(here, chain_all, 0.0), axis=1, keepdims=True)
        bins = jnp.where(
            own_chain == chain_all,
            jnp.clip(own_res - res_all + RELMAX, 0.0, 2.0 * RELMAX),
            2.0 * RELMAX + 1.0,
        ).astype(jnp.int32)
        table_t = jnp.concatenate(
            [table[...], jnp.zeros((HEADS, CLASSES - BINS), F32)], axis=1
        )
        high = table_t.astype(BF16)
        rest = table_t - high.astype(F32)
        middle = rest.astype(BF16)
        low = (rest - middle.astype(F32)).astype(BF16)
        classes = lax.broadcasted_iota(jnp.int32, (CLASSES, tokens), 0)
        for r in range(local):
            hot = jnp.where(classes == bins[r : r + 1, :], 1.0, 0.0).astype(BF16)
            bias[r] = dot(high, hot) + (dot(middle, hot) + dot(low, hot))

        for load in loads[4:11]:
            load.wait()
        half_wa = wa[...] * BF16(0.5)
        wpb_t = wpb[...]

        if chunks <= 8:
            for chunk in range(chunks):
                if chunk == chunks - 1:
                    answer()
                transition(chunk, half_wa, wpb_t)
        else:

            def body(chunk, carry):
                transition(chunk, half_wa, wpb_t)
                return carry

            lax.fori_loop(0, chunks, body, 0)
            answer()

    pl.when(is_early)(pair_work)

    @pl.when(is_late)
    def _():
        pl.semaphore_wait(barrier, devices - 1)
        for receiver in range(FRINGE):
            send(receiver, late_sem)
        repeat(FRINGE - 1, lambda step: send(last + other(me - last, step, FRINGE), late_sem))
        repeat(last - FRINGE, lambda step: send(FRINGE + step, late_sem))

    @pl.when(is_middle)
    def _():
        pl.semaphore_wait(barrier, last - 1)
        repeat(last - 1, lambda step: send(other(me, step, devices), recv_sem))

    @pl.when(is_early)
    def _():
        pl.semaphore_wait(barrier, devices - 1)
        repeat(FRINGE, lambda step: send(last + step, recv_sem))
        repeat(last - 1, lambda step: send(other(me, step, devices), recv_sem))

    pl.when(jnp.logical_not(is_early))(lambda: pair_work(answer))

    loads[11].wait()
    own = layer_norm(single[...].astype(F32)).astype(BF16)
    queries = dot(own, wp[:, :width]).astype(BF16).astype(F32)
    gates = dot(own, wp[:, 3 * width :]).astype(BF16).astype(F32)
    gates_ref[...] = jax.nn.sigmoid(gates)
    wv_ref[...] = wp[:, 2 * width : 3 * width]
    mine = own_columns(local, width)
    spread_queries = jnp.where(mine, queries[None, :, :], 0.0)
    spread_queries = spread_queries.reshape(HEADS * local, width).astype(BF16)
    spread_queries = dot_nt(spread_queries, wp[:, width : 2 * width]) * (
        1.0 / math.sqrt(HEAD_DIM)
    )
    spread_ref[...] = spread_queries.astype(BF16)
    for i in range(local):
        bias_ref[:, i, :] = bias[i]

    @pl.when(is_middle)
    def _():
        blocks(last - 1, recv_sem).wait_recv()

    @pl.when(is_late)
    def _():
        blocks(FRINGE - 1, late_sem).wait_recv()
        blocks(last, recv_sem).wait_recv()

    @pl.when(is_early)
    def _():
        blocks(last - 1, recv_sem).wait_recv()
        blocks(FRINGE, late_sem).wait_recv()

    blocks(devices - 1, recv_sem).wait_send()


def attention(
    new_pair_from,
    bias,
    keys,
    spread_queries,
    gates,
    wv,
    mask,
    wo,
    new_pair_ref,
    update_ref,
    update,
    out_sem,
    update_sem,
):
    local, width = gates.shape
    tokens = keys.shape[0]
    out = pltpu.make_async_copy(new_pair_from, new_pair_ref, out_sem)
    out.start()
    scores = dot_nt(spread_queries[...], keys[...])
    scores = scores + bias[...].reshape(HEADS * local, tokens)
    scores = jnp.where(mask[...] > 0, scores, -1000000000.0)
    expons = jnp.exp(scores - jnp.max(scores, axis=1, keepdims=True)).astype(BF16)
    values = dot(keys[...], wv[...]).astype(BF16)
    values = jnp.concatenate([values, jnp.ones((tokens, LANES), BF16)], axis=1)
    spread = dot(expons, values)
    shares = 1.0 / spread[:, width:]
    column = lax.broadcasted_iota(jnp.int32, (local, LANES), 1)
    pieces = []
    for first in range(0, width, LANES):
        piece = jnp.zeros((local, LANES), F32)
        for head in range(HEADS):
            begin, end = head * HEAD_DIM - first, (head + 1) * HEAD_DIM - first
            if begin < LANES and end > 0:
                rows = slice(head * local, (head + 1) * local)
                part = spread[rows, first : first + LANES] * shares[rows]
                piece = jnp.where((column >= begin) & (column < end), part, piece)
        pieces.append(piece)
    attended = jnp.concatenate(pieces, axis=1)
    gated = (gates[...] * attended).astype(BF16)
    update[...] = dot(gated, wo[...]).astype(BF16)
    done = pltpu.make_async_copy(update, update_ref, update_sem)
    done.start()
    done.wait()
    pltpu.make_async_copy(new_pair_from, new_pair_ref, out_sem).wait()


def on_device(
    devices,
    pair,
    single,
    token_mask,
    chain_index,
    residue_index,
    pair_gain,
    pair_norm_offset,
    w_swish_a,
    w_swish_b,
    w_trans_out,
    w_pair_bias,
    w_project,
    w_out,
    relative_position_bias,
):
    def line(vector):
        return vector.reshape(1, vector.shape[0])

    operands = (
        pair,
        single,
        line(chain_index),
        line(residue_index),
        line(pair_gain),
        line(pair_norm_offset),
        w_swish_a,
        w_swish_b,
        w_trans_out,
        w_pair_bias.T,
        w_project,
        relative_position_bias.T,
    )
    local, tokens, _ = pair.shape
    width = single.shape[1]
    anywhere = pl.BlockSpec(memory_space=pl.ANY)
    vmem = pl.BlockSpec(memory_space=pltpu.VMEM)
    held = [
        pltpu.VMEM(pair.shape, pair.dtype),
        pltpu.VMEM(single.shape, single.dtype),
        pltpu.VMEM((local, HEADS, tokens), F32),
    ]
    held += [pltpu.VMEM(x.shape, x.dtype) for x in operands[2:]]
    operands = [pltpu.with_memory_space_constraint(x, pltpu.HBM) for x in operands]
    handed = pl.pallas_call(
        functools.partial(kernel, devices),
        out_shape=(
            jax.ShapeDtypeStruct(pair.shape, BF16),
            jax.ShapeDtypeStruct((HEADS, local, tokens), F32),
            jax.ShapeDtypeStruct((tokens, width), BF16),
            jax.ShapeDtypeStruct((local * HEADS, width), BF16),
            jax.ShapeDtypeStruct((local, width), F32),
            jax.ShapeDtypeStruct((width, width), BF16),
        ),
        in_specs=[anywhere] * len(operands),
        out_specs=(vmem,) * 6,
        scratch_shapes=held
        + [
            pltpu.SemaphoreType.DMA((len(operands),)),
            pltpu.SemaphoreType.DMA,
            pltpu.SemaphoreType.DMA,
            pltpu.SemaphoreType.DMA,
        ],
        compiler_params=pltpu.CompilerParams(
            collective_id=0, has_side_effects=True, vmem_limit_bytes=GRANT
        ),
        name="pair_tail",
    )(*operands)
    return pl.pallas_call(
        attention,
        out_shape=(
            jax.ShapeDtypeStruct(pair.shape, BF16),
            jax.ShapeDtypeStruct(single.shape, BF16),
        ),
        in_specs=[anywhere] + [vmem] * 7,
        out_specs=(anywhere, anywhere),
        scratch_shapes=[pltpu.VMEM(single.shape, BF16), pltpu.SemaphoreType.DMA, pltpu.SemaphoreType.DMA],
        compiler_params=pltpu.CompilerParams(vmem_limit_bytes=GRANT),
        name="single_attention",
    )(*handed, line(token_mask), w_out)


def solution(mesh):
    rows = P(("groups", "row"))
    return jax.shard_map(
        functools.partial(on_device, mesh.shape["row"]),
        mesh=mesh,
        in_specs=(rows, rows) + (P("groups"),) * 3 + (P(),) * 9,
        out_specs=(rows, rows),
        check_vma=False,
    )
```

```python
import functools
import math

import jax
import jax.numpy as jnp
from jax import lax
from jax.experimental import pallas as pl
from jax.experimental.pallas import tpu as pltpu
from jax.sharding import PartitionSpec as P

HEADS = 16
HEAD_DIM = 24
RELMAX = 32
BINS = 66
CLASSES = 80
ROWS_AT_ONCE = 512
LANES = 128
FRINGE = 2
GRANT = 24 * 1024 * 1024

epsilon = 1e-05
F32 = jnp.float32
BF16 = jnp.bfloat16


def layer_norm(value_rows):
    middle = jnp.mean(value_rows, axis=-1, keepdims=True)
    centred = value_rows - middle
    spread = jnp.mean(centred * centred, axis=-1, keepdims=True)
    return centred * lax.rsqrt(spread + epsilon)


def dot(a, b):
    return jnp.dot(a, b, preferred_element_type=F32)


def dot_nt(a, b):
    return lax.dot_general(a, b, (((1,), (1,)), ((), ())), preferred_element_type=F32)


def other(me, step, devices):
    return step + (step - me + devices) // devices


def own_columns(local, width):
    place = lax.broadcasted_iota(jnp.int32, (HEADS, local, width), 2) - HEAD_DIM * (
        lax.broadcasted_iota(jnp.int32, (HEADS, local, width), 0)
    )
    return (place >= 0) & (place < HEAD_DIM)


def kernel(
    devices,
    pair_hbm,
    single_hbm,
    chain_hbm,
    res_hbm,
    gain_hbm,
    offset_hbm,
    wa_hbm,
    wb_hbm,
    wt_hbm,
    wpb_hbm,
    wp_hbm,
    table_hbm,
    new_pair_ref,
    bias_ref,
    keys_ref,
    stack_ref,
    gates_ref,
    pair,
    single,
    bias,
    chain,
    res,
    gain,
    offset,
    wa,
    wb,
    wt,
    wpb,
    wp,
    table,
    load_sem,
    send_sem,
    recv_sem,
    late_sem,
):
    me = lax.axis_index("row")
    local, tokens, channels = pair.shape
    width = single.shape[1]
    mine_at = pl.ds(pl.multiple_of(me * local, local), local)

    loads = [
        pltpu.make_async_copy(src, dst, load_sem.at[min(i, 1) + i // 11])
        for i, (src, dst) in enumerate(
            (
                (single_hbm, single),
                (chain_hbm, chain),
                (res_hbm, res),
                (table_hbm, table),
                (pair_hbm, pair),
                (gain_hbm, gain),
                (offset_hbm, offset),
                (wa_hbm, wa),
                (wb_hbm, wb),
                (wt_hbm, wt),
                (wpb_hbm, wpb),
                (wp_hbm, wp),
            )
        )
    ]
    barrier = pltpu.get_barrier_semaphore()

    last = devices - FRINGE
    is_early, is_late = me < FRINGE, me >= last
    is_middle = jnp.logical_not(jnp.logical_or(is_early, is_late))

    def repeat(count, act):
        def body(step, carry):
            act(step)
            return carry

        lax.fori_loop(0, count, body, 0, unroll=devices <= 16)

    def greet(receiver):
        pl.semaphore_signal(
            barrier,
            inc=1,
            device_id={"row": receiver},
            device_id_type=pl.DeviceIdType.MESH,
        )

    def send(receiver, arrival):
        pltpu.make_async_remote_copy(
            src_ref=keys_ref.at[mine_at],
            dst_ref=keys_ref.at[mine_at],
            send_sem=send_sem,
            recv_sem=arrival,
            device_id={"row": receiver},
            device_id_type=pl.DeviceIdType.MESH,
        ).start()

    def blocks(count, arrival):
        some = keys_ref.at[pl.ds(0, count * local)]
        return pltpu.make_async_remote_copy(
            src_ref=some,
            dst_ref=some,
            send_sem=send_sem,
            recv_sem=arrival,
            device_id={"row": other(me, 0, devices)},
            device_id_type=pl.DeviceIdType.MESH,
        )

    loads[0].start()

    @pl.when(is_late)
    def _():
        for receiver in range(FRINGE):
            greet(receiver)
        repeat(FRINGE - 1, lambda step: greet(last + other(me - last, step, FRINGE)))

    @pl.when(jnp.logical_not(is_late))
    def _():
        repeat(devices - 1, lambda step: greet(other(me, step, devices)))

    for load in loads[1:]:
        load.start()

    loads[0].wait()
    keys_ref[mine_at, :] = layer_norm(single[...].astype(F32)).astype(BF16)
    at_once = max(1, ROWS_AT_ONCE // tokens)
    span = min(tokens, ROWS_AT_ONCE)
    pieces = tokens // span

    def transition(chunk, half_wa, wpb_t):
        row = pl.ds((chunk // pieces) * at_once, at_once)
        start = (chunk % pieces) * span
        if not isinstance(start, int):
            start = pl.multiple_of(start, span)
        col = pl.ds(start, span)
        x = pair[row, col, :].reshape(at_once * span, channels).astype(F32)
        normed = (layer_norm(x) * gain[...] + offset[...]).astype(BF16)
        h = dot(normed, half_wa)
        second = dot(normed, wb[...])
        hidden = ((h + h * jnp.tanh(h)) * second).astype(BF16)
        updated = (x + dot(hidden, wt[...])).astype(BF16)
        new_pair_ref[row, col, :] = updated.reshape(at_once, span, channels)
        bias_input = layer_norm(updated.astype(F32)).astype(BF16)
        head_rows = dot_nt(wpb_t, bias_input).astype(BF16).astype(F32)
        for i in range(at_once):
            at = ((chunk // pieces) * at_once + i, slice(None), col)
            bias[at] = bias[at] + head_rows[:, i * span : (i + 1) * span]

    chunks = (local // at_once) * pieces
    def answer():
        @pl.when(is_middle)
        def _():
            blocks(FRINGE, late_sem).wait_recv()
            repeat(FRINGE, lambda step: send(last + step, recv_sem))

    def pair_work(answer=lambda: None):
        for load in loads[1:11]:
            load.wait()
        at = lax.broadcasted_iota(jnp.int32, (local, tokens), 1)
        own_at = lax.broadcasted_iota(jnp.int32, (local, tokens), 0) + me * local
        res_all = res[...].astype(F32)
        chain_all = chain[...].astype(F32)
        here = at == own_at
        own_res = jnp.sum(jnp.where(here, res_all, 0.0), axis=1, keepdims=True)
        own_chain = jnp.sum(jnp.where(here, chain_all, 0.0), axis=1, keepdims=True)
        bins = jnp.where(
            own_chain == chain_all,
            jnp.clip(own_res - res_all + RELMAX, 0.0, 2.0 * RELMAX),
            2.0 * RELMAX + 1.0,
        ).astype(jnp.int32)
        table_t = jnp.concatenate(
            [table[...], jnp.zeros((HEADS, CLASSES - BINS), F32)], axis=1
        )
        high = table_t.astype(BF16)
        rest = table_t - high.astype(F32)
        middle = rest.astype(BF16)
        low = (rest - middle.astype(F32)).astype(BF16)
        classes = lax.broadcasted_iota(jnp.int32, (CLASSES, tokens), 0)
        for r in range(local):
            hot = jnp.where(classes == bins[r : r + 1, :], 1.0, 0.0).astype(BF16)
            bias[r] = dot(high, hot) + (dot(middle, hot) + dot(low, hot))

        half_wa = wa[...] * BF16(0.5)
        wpb_t = wpb[...]

        if chunks <= 8:
            for chunk in range(chunks):
                if chunk == chunks - 1:
                    answer()
                transition(chunk, half_wa, wpb_t)
        else:

            def body(chunk, carry):
                transition(chunk, half_wa, wpb_t)
                return carry

            lax.fori_loop(0, chunks, body, 0)
            answer()

    pl.when(is_early)(pair_work)

    @pl.when(is_late)
    def _():
        pl.semaphore_wait(barrier, devices - 1)
        send(0, late_sem)
        repeat(4, lambda step: send(FRINGE + step, late_sem))
        send(1, late_sem)
        repeat(last - FRINGE - 4, lambda step: send(FRINGE + 4 + step, late_sem))
        repeat(FRINGE - 1, lambda step: send(last + other(me - last, step, FRINGE), late_sem))

    @pl.when(is_middle)
    def _():
        pl.semaphore_wait(barrier, last - 1)
        send(0, recv_sem)
        send(1, recv_sem)
        repeat(last - 1 - FRINGE, lambda step: send(other(me, last - 2 - step, devices), recv_sem))

    @pl.when(is_early)
    def _():
        pl.semaphore_wait(barrier, devices - 1)
        repeat(FRINGE, lambda step: send(last + step, recv_sem))
        repeat(last - 1, lambda step: send(other(me, step, devices), recv_sem))

    pl.when(jnp.logical_not(is_early))(lambda: pair_work(answer))

    loads[11].wait()
    own = layer_norm(single[...].astype(F32)).astype(BF16)
    queries = dot(own, wp[:, :width]).astype(BF16).astype(F32)
    gates = dot(own, wp[:, 3 * width :]).astype(BF16).astype(F32)
    gates_ref[...] = jax.nn.sigmoid(gates)
    values_t = wp[:, 2 * width : 3 * width].astype(F32).T.astype(BF16)
    stack_ref[HEADS * local :, :] = values_t
    mine = own_columns(local, width)
    spread_queries = jnp.where(mine, queries[None, :, :], 0.0)
    spread_queries = spread_queries.reshape(HEADS * local, width).astype(BF16)
    spread_queries = dot_nt(spread_queries, wp[:, width : 2 * width]) * (
        1.0 / math.sqrt(HEAD_DIM)
    )
    stack_ref[: HEADS * local, :] = spread_queries.astype(BF16)
    for i in range(local):
        bias_ref[:, i, :] = bias[i]

    @pl.when(is_middle)
    def _():
        blocks(last - 1, recv_sem).wait_recv()

    @pl.when(is_late)
    def _():
        blocks(FRINGE - 1, late_sem).wait_recv()
        blocks(last, recv_sem).wait_recv()

    @pl.when(is_early)
    def _():
        blocks(last - 1, recv_sem).wait_recv()
        blocks(FRINGE, late_sem).wait_recv()

    blocks(devices - 1, recv_sem).wait_send()


def attention(
    new_pair_from,
    bias,
    keys,
    stack,
    gates,
    mask,
    wo,
    new_pair_ref,
    update_ref,
    update,
    out_sem,
    update_sem,
):
    local, width = gates.shape
    tokens = keys.shape[0]
    out = pltpu.make_async_copy(new_pair_from, new_pair_ref, out_sem)
    out.start()
    both = dot_nt(stack[...], keys[...])
    scores = both[: HEADS * local] + bias[...].reshape(HEADS * local, tokens)
    scores = jnp.where(mask[...] > 0, scores, -1000000000.0)
    expons = jnp.exp(scores - jnp.max(scores, axis=1, keepdims=True)).astype(BF16)
    values_t = both[HEADS * local :].astype(BF16)
    ones = jnp.ones((LANES, tokens), BF16)
    column = lax.broadcasted_iota(jnp.int32, (local, LANES), 1)
    pieces = []
    for first in range(0, width, LANES):
        heads = range(first // HEAD_DIM, -(-(first + LANES) // HEAD_DIM))
        spread = dot_nt(
            expons[heads[0] * local : (heads[-1] + 1) * local],
            jnp.concatenate([values_t[first : first + LANES], ones], axis=0),
        )
        spread = spread[:, :LANES] / spread[:, LANES:]
        piece = spread[:local]
        for at, head in enumerate(heads[1:], 1):
            part = spread[at * local : (at + 1) * local]
            piece = jnp.where(column >= head * HEAD_DIM - first, part, piece)
        pieces.append(piece)
    attended = jnp.concatenate(pieces, axis=1)
    gated = (gates[...] * attended).astype(BF16)
    update[...] = dot(gated, wo[...]).astype(BF16)
    done = pltpu.make_async_copy(update, update_ref, update_sem)
    done.start()
    done.wait()
    pltpu.make_async_copy(new_pair_from, new_pair_ref, out_sem).wait()


def on_device(
    devices,
    pair,
    single,
    token_mask,
    chain_index,
    residue_index,
    pair_gain,
    pair_norm_offset,
    w_swish_a,
    w_swish_b,
    w_trans_out,
    w_pair_bias,
    w_project,
    w_out,
    relative_position_bias,
):
    def line(vector):
        return vector.reshape(1, vector.shape[0])

    operands = (
        pair,
        single,
        line(chain_index),
        line(residue_index),
        line(pair_gain),
        line(pair_norm_offset),
        w_swish_a,
        w_swish_b,
        w_trans_out,
        w_pair_bias.T,
        w_project,
        relative_position_bias.T,
    )
    local, tokens, _ = pair.shape
    width = single.shape[1]
    anywhere = pl.BlockSpec(memory_space=pl.ANY)
    vmem = pl.BlockSpec(memory_space=pltpu.VMEM)
    held = [
        pltpu.VMEM(pair.shape, pair.dtype),
        pltpu.VMEM(single.shape, single.dtype),
        pltpu.VMEM((local, HEADS, tokens), F32),
    ]
    held += [pltpu.VMEM(x.shape, x.dtype) for x in operands[2:]]
    operands = [pltpu.with_memory_space_constraint(x, pltpu.HBM) for x in operands]
    handed = pl.pallas_call(
        functools.partial(kernel, devices),
        out_shape=(
            jax.ShapeDtypeStruct(pair.shape, BF16),
            jax.ShapeDtypeStruct((HEADS, local, tokens), F32),
            jax.ShapeDtypeStruct((tokens, width), BF16),
            jax.ShapeDtypeStruct((HEADS * local + width, width), BF16),
            jax.ShapeDtypeStruct((local, width), F32),
        ),
        in_specs=[anywhere] * len(operands),
        out_specs=(vmem,) * 5,
        scratch_shapes=held
        + [
            pltpu.SemaphoreType.DMA((3,)),
            pltpu.SemaphoreType.DMA,
            pltpu.SemaphoreType.DMA,
            pltpu.SemaphoreType.DMA,
        ],
        compiler_params=pltpu.CompilerParams(
            collective_id=0, has_side_effects=True, vmem_limit_bytes=GRANT
        ),
        name="pair_tail",
    )(*operands)
    return pl.pallas_call(
        attention,
        out_shape=(
            jax.ShapeDtypeStruct(pair.shape, BF16),
            jax.ShapeDtypeStruct(single.shape, BF16),
        ),
        in_specs=[anywhere] + [vmem] * 6,
        out_specs=(anywhere, anywhere),
        scratch_shapes=[pltpu.VMEM(single.shape, BF16), pltpu.SemaphoreType.DMA, pltpu.SemaphoreType.DMA],
        compiler_params=pltpu.CompilerParams(vmem_limit_bytes=GRANT),
        name="single_attention",
    )(*handed, line(token_mask), w_out)


def solution(mesh):
    rows = P(("groups", "row"))
    return jax.shard_map(
        functools.partial(on_device, mesh.shape["row"]),
        mesh=mesh,
        in_specs=(rows, rows) + (P("groups"),) * 3 + (P(),) * 9,
        out_specs=(rows, rows),
        check_vma=False,
    )
```

```python
import functools
import math

import jax
import jax.numpy as jnp
from jax import lax
from jax.experimental import pallas as pl
from jax.experimental.pallas import tpu as pltpu
from jax.sharding import PartitionSpec as P

HEADS = 16
HEAD_DIM = 24
RELMAX = 32
BINS = 66
CLASSES = 80
ROWS_AT_ONCE = 512
LANES = 128
FRINGE = 2
GRANT = 24 * 1024 * 1024

epsilon = 1e-05
F32 = jnp.float32
BF16 = jnp.bfloat16


def layer_norm(value_rows):
    middle = jnp.mean(value_rows, axis=-1, keepdims=True)
    centred = value_rows - middle
    spread = jnp.mean(centred * centred, axis=-1, keepdims=True)
    return centred * lax.rsqrt(spread + epsilon)


def dot(a, b):
    return jnp.dot(a, b, preferred_element_type=F32)


def dot_nt(a, b):
    return lax.dot_general(a, b, (((1,), (1,)), ((), ())), preferred_element_type=F32)


def other(me, step, devices):
    return step + (step - me + devices) // devices


def own_columns(local, width):
    place = lax.broadcasted_iota(jnp.int32, (HEADS, local, width), 2) - HEAD_DIM * (
        lax.broadcasted_iota(jnp.int32, (HEADS, local, width), 0)
    )
    return (place >= 0) & (place < HEAD_DIM)


def kernel(
    devices,
    pair_hbm,
    single_hbm,
    chain_hbm,
    res_hbm,
    gain_hbm,
    offset_hbm,
    wa_hbm,
    wb_hbm,
    wt_hbm,
    wpb_hbm,
    wp_hbm,
    table_hbm,
    new_pair_ref,
    bias_ref,
    keys_ref,
    stack_ref,
    gates_ref,
    pair,
    single,
    bias,
    chain,
    res,
    gain,
    offset,
    wa,
    wb,
    wt,
    wpb,
    wp,
    table,
    load_sem,
    send_sem,
    recv_sem,
    late_sem,
):
    me = lax.axis_index("row")
    local, tokens, channels = pair.shape
    width = single.shape[1]
    mine_at = pl.ds(pl.multiple_of(me * local, local), local)

    loads = [
        pltpu.make_async_copy(src, dst, load_sem.at[min(i, 1) + i // 11])
        for i, (src, dst) in enumerate(
            (
                (single_hbm, single),
                (chain_hbm, chain),
                (res_hbm, res),
                (table_hbm, table),
                (pair_hbm, pair),
                (gain_hbm, gain),
                (offset_hbm, offset),
                (wa_hbm, wa),
                (wb_hbm, wb),
                (wt_hbm, wt),
                (wpb_hbm, wpb),
                (wp_hbm, wp),
            )
        )
    ]
    barrier = pltpu.get_barrier_semaphore()

    last = devices - FRINGE
    is_early, is_late = me < FRINGE, me >= last
    is_middle = jnp.logical_not(jnp.logical_or(is_early, is_late))

    def repeat(count, act):
        def body(step, carry):
            act(step)
            return carry

        lax.fori_loop(0, count, body, 0, unroll=devices <= 16)

    def greet(receiver):
        pl.semaphore_signal(
            barrier,
            inc=1,
            device_id={"row": receiver},
            device_id_type=pl.DeviceIdType.MESH,
        )

    def send(receiver, arrival):
        pltpu.make_async_remote_copy(
            src_ref=keys_ref.at[mine_at],
            dst_ref=keys_ref.at[mine_at],
            send_sem=send_sem,
            recv_sem=arrival,
            device_id={"row": receiver},
            device_id_type=pl.DeviceIdType.MESH,
        ).start()

    def blocks(count, arrival):
        some = keys_ref.at[pl.ds(0, count * local)]
        return pltpu.make_async_remote_copy(
            src_ref=some,
            dst_ref=some,
            send_sem=send_sem,
            recv_sem=arrival,
            device_id={"row": other(me, 0, devices)},
            device_id_type=pl.DeviceIdType.MESH,
        )

    loads[0].start()

    @pl.when(is_late)
    def _():
        for receiver in range(FRINGE):
            greet(receiver)
        repeat(FRINGE - 1, lambda step: greet(last + other(me - last, step, FRINGE)))

    @pl.when(jnp.logical_not(is_late))
    def _():
        repeat(devices - 1, lambda step: greet(other(me, step, devices)))

    for load in loads[1:]:
        load.start()

    loads[0].wait()
    keys_ref[mine_at, :] = layer_norm(single[...].astype(F32)).astype(BF16)
    at_once = max(1, ROWS_AT_ONCE // tokens)
    span = min(tokens, ROWS_AT_ONCE)
    pieces = tokens // span

    def transition(chunk, half_wa, wpb_t):
        row = pl.ds((chunk // pieces) * at_once, at_once)
        start = (chunk % pieces) * span
        if not isinstance(start, int):
            start = pl.multiple_of(start, span)
        col = pl.ds(start, span)
        x = pair[row, col, :].reshape(at_once * span, channels).astype(F32)
        normed = (layer_norm(x) * gain[...] + offset[...]).astype(BF16)
        h = dot(normed, half_wa)
        second = dot(normed, wb[...])
        hidden = ((h + h * jnp.tanh(h)) * second).astype(BF16)
        updated = (x + dot(hidden, wt[...])).astype(BF16)
        new_pair_ref[row, col, :] = updated.reshape(at_once, span, channels)
        bias_input = layer_norm(updated.astype(F32)).astype(BF16)
        head_rows = dot_nt(wpb_t, bias_input).astype(BF16).astype(F32)
        for i in range(at_once):
            at = ((chunk // pieces) * at_once + i, slice(None), col)
            bias[at] = bias[at] + head_rows[:, i * span : (i + 1) * span]

    chunks = (local // at_once) * pieces
    def answer():
        @pl.when(is_middle)
        def _():
            blocks(FRINGE, late_sem).wait_recv()
            repeat(FRINGE, lambda step: send(last + step, recv_sem))

    def pair_work(answer=lambda: None):
        for load in loads[1:11]:
            load.wait()
        at = lax.broadcasted_iota(jnp.int32, (local, tokens), 1)
        own_at = lax.broadcasted_iota(jnp.int32, (local, tokens), 0) + me * local
        res_all = res[...].astype(F32)
        chain_all = chain[...].astype(F32)
        here = at == own_at
        own_res = jnp.sum(jnp.where(here, res_all, 0.0), axis=1, keepdims=True)
        own_chain = jnp.sum(jnp.where(here, chain_all, 0.0), axis=1, keepdims=True)
        bins = jnp.where(
            own_chain == chain_all,
            jnp.clip(own_res - res_all + RELMAX, 0.0, 2.0 * RELMAX),
            2.0 * RELMAX + 1.0,
        ).astype(jnp.int32)
        table_t = jnp.concatenate(
            [table[...], jnp.zeros((HEADS, CLASSES - BINS), F32)], axis=1
        )
        high = table_t.astype(BF16)
        rest = table_t - high.astype(F32)
        middle = rest.astype(BF16)
        low = (rest - middle.astype(F32)).astype(BF16)
        classes = lax.broadcasted_iota(jnp.int32, (CLASSES, tokens), 0)
        for r in range(local):
            hot = jnp.where(classes == bins[r : r + 1, :], 1.0, 0.0).astype(BF16)
            bias[r] = dot(high, hot) + (dot(middle, hot) + dot(low, hot))

        half_wa = wa[...] * BF16(0.5)
        wpb_t = wpb[...]

        if chunks <= 8:
            for chunk in range(chunks):
                if chunk == chunks - 1:
                    answer()
                transition(chunk, half_wa, wpb_t)
        else:

            def body(chunk, carry):
                transition(chunk, half_wa, wpb_t)
                return carry

            lax.fori_loop(0, chunks, body, 0)
            answer()

    pl.when(is_early)(pair_work)

    @pl.when(is_late)
    def _():
        pl.semaphore_wait(barrier, devices - 1)
        send(0, late_sem)
        repeat(4, lambda step: send(FRINGE + step, late_sem))
        send(1, late_sem)
        repeat(last - FRINGE - 4, lambda step: send(FRINGE + 4 + step, late_sem))
        repeat(FRINGE - 1, lambda step: send(last + other(me - last, step, FRINGE), late_sem))

    @pl.when(is_middle)
    def _():
        pl.semaphore_wait(barrier, last - 1)
        send(0, recv_sem)
        send(1, recv_sem)
        repeat(last - 1 - FRINGE, lambda step: send(other(me, last - 2 - step, devices), recv_sem))

    @pl.when(is_early)
    def _():
        pl.semaphore_wait(barrier, devices - 1)
        repeat(FRINGE, lambda step: send(last + step, recv_sem))
        repeat(last - 1, lambda step: send(other(me, step, devices), recv_sem))

    pl.when(jnp.logical_not(is_early))(lambda: pair_work(answer))

    loads[11].wait()
    own = layer_norm(single[...].astype(F32)).astype(BF16)
    queries = dot(own, wp[:, :width]).astype(BF16).astype(F32)
    gates = dot(own, wp[:, 3 * width :]).astype(BF16).astype(F32)
    gates_ref[...] = jax.nn.sigmoid(gates)
    values_t = wp[:, 2 * width : 3 * width].astype(F32).T.astype(BF16)
    stack_ref[HEADS * local :, :] = values_t
    mine = own_columns(local, width)
    spread_queries = jnp.where(mine, queries[None, :, :], 0.0)
    spread_queries = spread_queries.reshape(HEADS * local, width).astype(BF16)
    spread_queries = dot_nt(spread_queries, wp[:, width : 2 * width]) * (
        1.0 / math.sqrt(HEAD_DIM)
    )
    stack_ref[: HEADS * local, :] = spread_queries.astype(BF16)
    for i in range(local):
        bias_ref[:, i, :] = bias[i]

    @pl.when(is_middle)
    def _():
        blocks(last - 1, recv_sem).wait_recv()

    @pl.when(is_late)
    def _():
        blocks(FRINGE - 1, late_sem).wait_recv()
        blocks(last, recv_sem).wait_recv()

    @pl.when(is_early)
    def _():
        blocks(last - 1, recv_sem).wait_recv()
        blocks(FRINGE, late_sem).wait_recv()

    blocks(devices - 1, recv_sem).wait_send()


def attention(
    new_pair_from,
    bias,
    keys,
    stack,
    gates,
    mask,
    wo,
    new_pair_ref,
    update_ref,
    update,
    out_sem,
    update_sem,
):
    local, width = gates.shape
    tokens = keys.shape[0]
    out = pltpu.make_async_copy(new_pair_from, new_pair_ref, out_sem)
    out.start()
    both = dot_nt(stack[...], keys[...])
    scores = both[: HEADS * local] + bias[...].reshape(HEADS * local, tokens)
    scores = jnp.where(mask[...] > 0, scores, -1000000000.0)
    expons = jnp.exp(scores - jnp.max(scores, axis=1, keepdims=True)).astype(BF16)
    values_t = both[HEADS * local :].astype(BF16)
    ones = jnp.ones((LANES, tokens), BF16)
    column = lax.broadcasted_iota(jnp.int32, (local, LANES), 1)
    pieces = []
    for first in range(0, width, LANES):
        heads = range(first // HEAD_DIM, -(-(first + LANES) // HEAD_DIM))
        spread = dot_nt(
            expons[heads[0] * local : (heads[-1] + 1) * local],
            jnp.concatenate([values_t[first : first + LANES], ones], axis=0),
        )
        own = spread[:local]
        for at, head in enumerate(heads[1:], 1):
            part = spread[at * local : (at + 1) * local]
            reached = jnp.concatenate([column, column], axis=1) >= head * HEAD_DIM - first
            own = jnp.where(reached, part, own)
        piece = own[:, :LANES] / own[:, LANES:]
        pieces.append(piece)
    attended = jnp.concatenate(pieces, axis=1)
    gated = (gates[...] * attended).astype(BF16)
    update[...] = dot(gated, wo[...]).astype(BF16)
    done = pltpu.make_async_copy(update, update_ref, update_sem)
    done.start()
    done.wait()
    pltpu.make_async_copy(new_pair_from, new_pair_ref, out_sem).wait()


def on_device(
    devices,
    pair,
    single,
    token_mask,
    chain_index,
    residue_index,
    pair_gain,
    pair_norm_offset,
    w_swish_a,
    w_swish_b,
    w_trans_out,
    w_pair_bias,
    w_project,
    w_out,
    relative_position_bias,
):
    def line(vector):
        return vector.reshape(1, vector.shape[0])

    operands = (
        pair,
        single,
        line(chain_index),
        line(residue_index),
        line(pair_gain),
        line(pair_norm_offset),
        w_swish_a,
        w_swish_b,
        w_trans_out,
        w_pair_bias.T,
        w_project,
        relative_position_bias.T,
    )
    local, tokens, _ = pair.shape
    width = single.shape[1]
    anywhere = pl.BlockSpec(memory_space=pl.ANY)
    vmem = pl.BlockSpec(memory_space=pltpu.VMEM)
    held = [
        pltpu.VMEM(pair.shape, pair.dtype),
        pltpu.VMEM(single.shape, single.dtype),
        pltpu.VMEM((local, HEADS, tokens), F32),
    ]
    held += [pltpu.VMEM(x.shape, x.dtype) for x in operands[2:]]
    operands = [pltpu.with_memory_space_constraint(x, pltpu.HBM) for x in operands]
    handed = pl.pallas_call(
        functools.partial(kernel, devices),
        out_shape=(
            jax.ShapeDtypeStruct(pair.shape, BF16),
            jax.ShapeDtypeStruct((HEADS, local, tokens), F32),
            jax.ShapeDtypeStruct((tokens, width), BF16),
            jax.ShapeDtypeStruct((HEADS * local + width, width), BF16),
            jax.ShapeDtypeStruct((local, width), F32),
        ),
        in_specs=[anywhere] * len(operands),
        out_specs=(vmem,) * 5,
        scratch_shapes=held
        + [
            pltpu.SemaphoreType.DMA((3,)),
            pltpu.SemaphoreType.DMA,
            pltpu.SemaphoreType.DMA,
            pltpu.SemaphoreType.DMA,
        ],
        compiler_params=pltpu.CompilerParams(
            collective_id=0, has_side_effects=True, vmem_limit_bytes=GRANT
        ),
        name="pair_tail",
    )(*operands)
    return pl.pallas_call(
        attention,
        out_shape=(
            jax.ShapeDtypeStruct(pair.shape, BF16),
            jax.ShapeDtypeStruct(single.shape, BF16),
        ),
        in_specs=[anywhere] + [vmem] * 6,
        out_specs=(anywhere, anywhere),
        scratch_shapes=[pltpu.VMEM(single.shape, BF16), pltpu.SemaphoreType.DMA, pltpu.SemaphoreType.DMA],
        compiler_params=pltpu.CompilerParams(vmem_limit_bytes=GRANT),
        name="single_attention",
    )(*handed, line(token_mask), w_out)


def solution(mesh):
    rows = P(("groups", "row"))
    return jax.shard_map(
        functools.partial(on_device, mesh.shape["row"]),
        mesh=mesh,
        in_specs=(rows, rows) + (P("groups"),) * 3 + (P(),) * 9,
        out_specs=(rows, rows),
        check_vma=False,
    )
```

```python
import functools
import math

import jax
import jax.numpy as jnp
from jax import lax
from jax.experimental import pallas as pl
from jax.experimental.pallas import tpu as pltpu
from jax.sharding import PartitionSpec as P

HEADS = 16
HEAD_DIM = 24
RELMAX = 32
BINS = 66
CLASSES = 80
ROWS_AT_ONCE = 512
LANES = 128
LOG2E = 1.0 / math.log(2.0)
FRINGE = 2
GRANT = 24 * 1024 * 1024

epsilon = 1e-05
F32 = jnp.float32
BF16 = jnp.bfloat16


def layer_norm(value_rows):
    middle = jnp.mean(value_rows, axis=-1, keepdims=True)
    centred = value_rows - middle
    spread = jnp.mean(centred * centred, axis=-1, keepdims=True)
    return centred * lax.rsqrt(spread + epsilon)


def dot(a, b):
    return jnp.dot(a, b, preferred_element_type=F32)


def dot_nt(a, b):
    return lax.dot_general(a, b, (((1,), (1,)), ((), ())), preferred_element_type=F32)


def other(me, step, devices):
    return step + (step - me + devices) // devices


def own_columns(local, width):
    place = lax.broadcasted_iota(jnp.int32, (HEADS, local, width), 2) - HEAD_DIM * (
        lax.broadcasted_iota(jnp.int32, (HEADS, local, width), 0)
    )
    return (place >= 0) & (place < HEAD_DIM)


def kernel(
    devices,
    pair_hbm,
    single_hbm,
    chain_hbm,
    res_hbm,
    gain_hbm,
    offset_hbm,
    wa_hbm,
    wb_hbm,
    wt_hbm,
    wpb_hbm,
    wp_hbm,
    table_hbm,
    new_pair_ref,
    bias_ref,
    keys_ref,
    stack_ref,
    gates_ref,
    pair,
    single,
    bias,
    chain,
    res,
    gain,
    offset,
    wa,
    wb,
    wt,
    wpb,
    wp,
    table,
    load_sem,
    send_sem,
    recv_sem,
    late_sem,
):
    me = lax.axis_index("row")
    local, tokens, channels = pair.shape
    width = single.shape[1]
    mine_at = pl.ds(pl.multiple_of(me * local, local), local)

    loads = [
        pltpu.make_async_copy(src, dst, load_sem.at[min(i, 1) + i // 11])
        for i, (src, dst) in enumerate(
            (
                (single_hbm, single),
                (chain_hbm, chain),
                (res_hbm, res),
                (table_hbm, table),
                (pair_hbm, pair),
                (gain_hbm, gain),
                (offset_hbm, offset),
                (wa_hbm, wa),
                (wb_hbm, wb),
                (wt_hbm, wt),
                (wpb_hbm, wpb),
                (wp_hbm, wp),
            )
        )
    ]
    barrier = pltpu.get_barrier_semaphore()

    last = devices - FRINGE
    is_early, is_late = me < FRINGE, me >= last
    is_middle = jnp.logical_not(jnp.logical_or(is_early, is_late))

    def repeat(count, act):
        def body(step, carry):
            act(step)
            return carry

        lax.fori_loop(0, count, body, 0, unroll=devices <= 16)

    def greet(receiver):
        pl.semaphore_signal(
            barrier,
            inc=1,
            device_id={"row": receiver},
            device_id_type=pl.DeviceIdType.MESH,
        )

    def send(receiver, arrival):
        pltpu.make_async_remote_copy(
            src_ref=keys_ref.at[mine_at],
            dst_ref=keys_ref.at[mine_at],
            send_sem=send_sem,
            recv_sem=arrival,
            device_id={"row": receiver},
            device_id_type=pl.DeviceIdType.MESH,
        ).start()

    def blocks(count, arrival):
        some = keys_ref.at[pl.ds(0, count * local)]
        return pltpu.make_async_remote_copy(
            src_ref=some,
            dst_ref=some,
            send_sem=send_sem,
            recv_sem=arrival,
            device_id={"row": other(me, 0, devices)},
            device_id_type=pl.DeviceIdType.MESH,
        )

    loads[0].start()

    @pl.when(is_late)
    def _():
        for receiver in range(FRINGE):
            greet(receiver)
        repeat(FRINGE - 1, lambda step: greet(last + other(me - last, step, FRINGE)))

    @pl.when(jnp.logical_not(is_late))
    def _():
        repeat(devices - 1, lambda step: greet(other(me, step, devices)))

    for load in loads[1:]:
        load.start()

    loads[0].wait()
    keys_ref[mine_at, :] = layer_norm(single[...].astype(F32)).astype(BF16)
    at_once = max(1, ROWS_AT_ONCE // tokens)
    span = min(tokens, ROWS_AT_ONCE)
    pieces = tokens // span

    def transition(chunk, half_wa, wpb_t):
        row = pl.ds((chunk // pieces) * at_once, at_once)
        start = (chunk % pieces) * span
        if not isinstance(start, int):
            start = pl.multiple_of(start, span)
        col = pl.ds(start, span)
        x = pair[row, col, :].reshape(at_once * span, channels).astype(F32)
        normed = (layer_norm(x) * gain[...] + offset[...]).astype(BF16)
        h = dot(normed, half_wa)
        second = dot(normed, wb[...])
        hidden = ((h + h * jnp.tanh(h)) * second).astype(BF16)
        updated = (x + dot(hidden, wt[...])).astype(BF16)
        new_pair_ref[row, col, :] = updated.reshape(at_once, span, channels)
        bias_input = layer_norm(updated.astype(F32)).astype(BF16)
        head_rows = dot_nt(wpb_t, bias_input).astype(BF16).astype(F32)
        for i in range(at_once):
            at = ((chunk // pieces) * at_once + i, slice(None), col)
            bias[at] = bias[at] + head_rows[:, i * span : (i + 1) * span]

    chunks = (local // at_once) * pieces
    def answer():
        @pl.when(is_middle)
        def _():
            blocks(FRINGE, late_sem).wait_recv()
            repeat(FRINGE, lambda step: send(last + step, recv_sem))

    def pair_work(answer=lambda: None):
        for load in loads[1:11]:
            load.wait()
        at = lax.broadcasted_iota(jnp.int32, (local, tokens), 1)
        own_at = lax.broadcasted_iota(jnp.int32, (local, tokens), 0) + me * local
        res_all = res[...].astype(F32)
        chain_all = chain[...].astype(F32)
        here = at == own_at
        own_res = jnp.sum(jnp.where(here, res_all, 0.0), axis=1, keepdims=True)
        own_chain = jnp.sum(jnp.where(here, chain_all, 0.0), axis=1, keepdims=True)
        bins = jnp.where(
            own_chain == chain_all,
            jnp.clip(own_res - res_all + RELMAX, 0.0, 2.0 * RELMAX),
            2.0 * RELMAX + 1.0,
        ).astype(jnp.int32)
        table_t = jnp.concatenate(
            [table[...], jnp.zeros((HEADS, CLASSES - BINS), F32)], axis=1
        )
        high = table_t.astype(BF16)
        rest = table_t - high.astype(F32)
        middle = rest.astype(BF16)
        low = (rest - middle.astype(F32)).astype(BF16)
        classes = lax.broadcasted_iota(jnp.int32, (CLASSES, tokens), 0)
        for r in range(local):
            hot = jnp.where(classes == bins[r : r + 1, :], 1.0, 0.0).astype(BF16)
            bias[r] = dot(high, hot) + (dot(middle, hot) + dot(low, hot))

        half_wa = wa[...] * BF16(0.5)
        wpb_t = wpb[...]

        if chunks <= 8:
            for chunk in range(chunks):
                if chunk == chunks - 1:
                    answer()
                transition(chunk, half_wa, wpb_t)
        else:

            def body(chunk, carry):
                transition(chunk, half_wa, wpb_t)
                return carry

            lax.fori_loop(0, chunks, body, 0)
            answer()

    pl.when(is_early)(pair_work)

    @pl.when(is_late)
    def _():
        pl.semaphore_wait(barrier, devices - 1)
        send(0, late_sem)
        repeat(4, lambda step: send(FRINGE + step, late_sem))
        send(1, late_sem)
        repeat(last - FRINGE - 4, lambda step: send(FRINGE + 4 + step, late_sem))
        repeat(FRINGE - 1, lambda step: send(last + other(me - last, step, FRINGE), late_sem))

    @pl.when(is_middle)
    def _():
        pl.semaphore_wait(barrier, last - 1)
        send(0, recv_sem)
        send(1, recv_sem)
        repeat(last - 1 - FRINGE, lambda step: send(other(me, last - 2 - step, devices), recv_sem))

    @pl.when(is_early)
    def _():
        pl.semaphore_wait(barrier, devices - 1)
        repeat(FRINGE, lambda step: send(last + step, recv_sem))
        repeat(last - 1, lambda step: send(other(me, step, devices), recv_sem))

    pl.when(jnp.logical_not(is_early))(lambda: pair_work(answer))

    loads[11].wait()
    own = layer_norm(single[...].astype(F32)).astype(BF16)
    queries = dot(own, wp[:, :width]).astype(BF16).astype(F32)
    gates = dot(own, wp[:, 3 * width :]).astype(BF16).astype(F32)
    gates_ref[...] = jax.nn.sigmoid(gates)
    values_t = wp[:, 2 * width : 3 * width].astype(F32).T.astype(BF16)
    stack_ref[HEADS * local :, :] = values_t
    mine = own_columns(local, width)
    spread_queries = jnp.where(mine, queries[None, :, :], 0.0)
    spread_queries = spread_queries.reshape(HEADS * local, width).astype(BF16)
    spread_queries = dot_nt(spread_queries, wp[:, width : 2 * width]) * (
        LOG2E / math.sqrt(HEAD_DIM)
    )
    stack_ref[: HEADS * local, :] = spread_queries.astype(BF16)
    for i in range(local):
        bias_ref[:, i, :] = bias[i] * LOG2E

    @pl.when(is_middle)
    def _():
        blocks(last - 1, recv_sem).wait_recv()

    @pl.when(is_late)
    def _():
        blocks(FRINGE - 1, late_sem).wait_recv()
        blocks(last, recv_sem).wait_recv()

    @pl.when(is_early)
    def _():
        blocks(last - 1, recv_sem).wait_recv()
        blocks(FRINGE, late_sem).wait_recv()

    blocks(devices - 1, recv_sem).wait_send()


def attention(
    new_pair_from,
    bias,
    keys,
    stack,
    gates,
    mask,
    wo,
    new_pair_ref,
    update_ref,
    update,
    out_sem,
    update_sem,
):
    local, width = gates.shape
    tokens = keys.shape[0]
    out = pltpu.make_async_copy(new_pair_from, new_pair_ref, out_sem)
    out.start()
    both = dot_nt(stack[...], keys[...])
    scores = both[: HEADS * local] + bias[...].reshape(HEADS * local, tokens)
    scores = jnp.where(mask[...] > 0, scores, -1000000000.0 * LOG2E)
    expons = jnp.exp2(scores - jnp.max(scores, axis=1, keepdims=True)).astype(BF16)
    values_t = both[HEADS * local :].astype(BF16)
    ones = jnp.ones((LANES, tokens), BF16)
    column = lax.broadcasted_iota(jnp.int32, (local, LANES), 1)
    pieces = []
    for first in range(0, width, LANES):
        heads = range(first // HEAD_DIM, -(-(first + LANES) // HEAD_DIM))
        spread = dot_nt(
            expons[heads[0] * local : (heads[-1] + 1) * local],
            jnp.concatenate([values_t[first : first + LANES], ones], axis=0),
        )
        own = spread[:local]
        for at, head in enumerate(heads[1:], 1):
            part = spread[at * local : (at + 1) * local]
            reached = jnp.concatenate([column, column], axis=1) >= head * HEAD_DIM - first
            own = jnp.where(reached, part, own)
        piece = own[:, :LANES] / own[:, LANES:]
        pieces.append(piece)
    attended = jnp.concatenate(pieces, axis=1)
    gated = (gates[...] * attended).astype(BF16)
    update[...] = dot(gated, wo[...]).astype(BF16)
    done = pltpu.make_async_copy(update, update_ref, update_sem)
    done.start()
    done.wait()
    pltpu.make_async_copy(new_pair_from, new_pair_ref, out_sem).wait()


def on_device(
    devices,
    pair,
    single,
    token_mask,
    chain_index,
    residue_index,
    pair_gain,
    pair_norm_offset,
    w_swish_a,
    w_swish_b,
    w_trans_out,
    w_pair_bias,
    w_project,
    w_out,
    relative_position_bias,
):
    def line(vector):
        return vector.reshape(1, vector.shape[0])

    operands = (
        pair,
        single,
        line(chain_index),
        line(residue_index),
        line(pair_gain),
        line(pair_norm_offset),
        w_swish_a,
        w_swish_b,
        w_trans_out,
        w_pair_bias.T,
        w_project,
        relative_position_bias.T,
    )
    local, tokens, _ = pair.shape
    width = single.shape[1]
    anywhere = pl.BlockSpec(memory_space=pl.ANY)
    vmem = pl.BlockSpec(memory_space=pltpu.VMEM)
    held = [
        pltpu.VMEM(pair.shape, pair.dtype),
        pltpu.VMEM(single.shape, single.dtype),
        pltpu.VMEM((local, HEADS, tokens), F32),
    ]
    held += [pltpu.VMEM(x.shape, x.dtype) for x in operands[2:]]
    operands = [pltpu.with_memory_space_constraint(x, pltpu.HBM) for x in operands]
    handed = pl.pallas_call(
        functools.partial(kernel, devices),
        out_shape=(
            jax.ShapeDtypeStruct(pair.shape, BF16),
            jax.ShapeDtypeStruct((HEADS, local, tokens), F32),
            jax.ShapeDtypeStruct((tokens, width), BF16),
            jax.ShapeDtypeStruct((HEADS * local + width, width), BF16),
            jax.ShapeDtypeStruct((local, width), F32),
        ),
        in_specs=[anywhere] * len(operands),
        out_specs=(vmem,) * 5,
        scratch_shapes=held
        + [
            pltpu.SemaphoreType.DMA((3,)),
            pltpu.SemaphoreType.DMA,
            pltpu.SemaphoreType.DMA,
            pltpu.SemaphoreType.DMA,
        ],
        compiler_params=pltpu.CompilerParams(
            collective_id=0, has_side_effects=True, vmem_limit_bytes=GRANT
        ),
        name="pair_tail",
    )(*operands)
    return pl.pallas_call(
        attention,
        out_shape=(
            jax.ShapeDtypeStruct(pair.shape, BF16),
            jax.ShapeDtypeStruct(single.shape, BF16),
        ),
        in_specs=[anywhere] + [vmem] * 6,
        out_specs=(anywhere, anywhere),
        scratch_shapes=[pltpu.VMEM(single.shape, BF16), pltpu.SemaphoreType.DMA, pltpu.SemaphoreType.DMA],
        compiler_params=pltpu.CompilerParams(vmem_limit_bytes=GRANT),
        name="single_attention",
    )(*handed, line(token_mask), w_out)


def solution(mesh):
    rows = P(("groups", "row"))
    return jax.shard_map(
        functools.partial(on_device, mesh.shape["row"]),
        mesh=mesh,
        in_specs=(rows, rows) + (P("groups"),) * 3 + (P(),) * 9,
        out_specs=(rows, rows),
        check_vma=False,
    )
```

```python
import functools
import math

import jax
import jax.numpy as jnp
from jax import lax
from jax.experimental import pallas as pl
from jax.experimental.pallas import tpu as pltpu
from jax.sharding import PartitionSpec as P

HEADS = 16
HEAD_DIM = 24
RELMAX = 32
BINS = 66
CLASSES = 80
ROWS_AT_ONCE = 512
LANES = 128
FRINGE = 2
GRANT = 24 * 1024 * 1024

epsilon = 1e-05
F32 = jnp.float32
BF16 = jnp.bfloat16


def layer_norm(value_rows):
    middle = jnp.mean(value_rows, axis=-1, keepdims=True)
    centred = value_rows - middle
    spread = jnp.mean(centred * centred, axis=-1, keepdims=True)
    return centred * lax.rsqrt(spread + epsilon)


def dot(a, b):
    return jnp.dot(a, b, preferred_element_type=F32)


def dot_nt(a, b):
    return lax.dot_general(a, b, (((1,), (1,)), ((), ())), preferred_element_type=F32)


def other(me, step, devices):
    return step + (step - me + devices) // devices


def own_columns(local, width):
    place = lax.broadcasted_iota(jnp.int32, (HEADS, local, width), 2) - HEAD_DIM * (
        lax.broadcasted_iota(jnp.int32, (HEADS, local, width), 0)
    )
    return (place >= 0) & (place < HEAD_DIM)


def kernel(
    devices,
    pair_hbm,
    single_hbm,
    chain_hbm,
    res_hbm,
    gain_hbm,
    offset_hbm,
    wa_hbm,
    wb_hbm,
    wt_hbm,
    wpb_hbm,
    wp_hbm,
    table_hbm,
    new_pair_ref,
    bias_ref,
    keys_ref,
    stack_ref,
    gates_ref,
    pair,
    single,
    bias,
    chain,
    res,
    gain,
    offset,
    wa,
    wb,
    wt,
    wpb,
    wp,
    table,
    load_sem,
    send_sem,
    recv_sem,
    late_sem,
):
    me = lax.axis_index("row")
    local, tokens, channels = pair.shape
    width = single.shape[1]
    mine_at = pl.ds(pl.multiple_of(me * local, local), local)

    loads = [
        pltpu.make_async_copy(src, dst, load_sem.at[min(i, 1) + i // 11])
        for i, (src, dst) in enumerate(
            (
                (single_hbm, single),
                (chain_hbm, chain),
                (res_hbm, res),
                (table_hbm, table),
                (pair_hbm, pair),
                (gain_hbm, gain),
                (offset_hbm, offset),
                (wa_hbm, wa),
                (wb_hbm, wb),
                (wt_hbm, wt),
                (wpb_hbm, wpb),
                (wp_hbm, wp),
            )
        )
    ]
    barrier = pltpu.get_barrier_semaphore()

    last = devices - FRINGE
    is_early, is_late = me < FRINGE, me >= last
    is_middle = jnp.logical_not(jnp.logical_or(is_early, is_late))

    def repeat(count, act):
        def body(step, carry):
            act(step)
            return carry

        lax.fori_loop(0, count, body, 0, unroll=devices <= 16)

    def greet(receiver):
        pl.semaphore_signal(
            barrier,
            inc=1,
            device_id={"row": receiver},
            device_id_type=pl.DeviceIdType.MESH,
        )

    def send(receiver, arrival):
        pltpu.make_async_remote_copy(
            src_ref=keys_ref.at[mine_at],
            dst_ref=keys_ref.at[mine_at],
            send_sem=send_sem,
            recv_sem=arrival,
            device_id={"row": receiver},
            device_id_type=pl.DeviceIdType.MESH,
        ).start()

    def blocks(count, arrival):
        some = keys_ref.at[pl.ds(0, count * local)]
        return pltpu.make_async_remote_copy(
            src_ref=some,
            dst_ref=some,
            send_sem=send_sem,
            recv_sem=arrival,
            device_id={"row": other(me, 0, devices)},
            device_id_type=pl.DeviceIdType.MESH,
        )

    loads[0].start()

    @pl.when(is_late)
    def _():
        for receiver in range(FRINGE):
            greet(receiver)
        repeat(FRINGE - 1, lambda step: greet(last + other(me - last, step, FRINGE)))

    @pl.when(jnp.logical_not(is_late))
    def _():
        repeat(devices - 1 - FRINGE, lambda step: greet(other(me, step + FRINGE, devices)))
        repeat(FRINGE, lambda step: greet(other(me, step, devices)))

    for load in loads[1:]:
        load.start()

    loads[0].wait()
    keys_ref[mine_at, :] = layer_norm(single[...].astype(F32)).astype(BF16)
    at_once = max(1, ROWS_AT_ONCE // tokens)
    span = min(tokens, ROWS_AT_ONCE)
    pieces = tokens // span

    def transition(chunk, half_wa, wpb_t):
        row = pl.ds((chunk // pieces) * at_once, at_once)
        start = (chunk % pieces) * span
        if not isinstance(start, int):
            start = pl.multiple_of(start, span)
        col = pl.ds(start, span)
        x = pair[row, col, :].reshape(at_once * span, channels).astype(F32)
        normed = (layer_norm(x) * gain[...] + offset[...]).astype(BF16)
        h = dot(normed, half_wa)
        second = dot(normed, wb[...])
        hidden = ((h + h * jnp.tanh(h)) * second).astype(BF16)
        updated = (x + dot(hidden, wt[...])).astype(BF16)
        new_pair_ref[row, col, :] = updated.reshape(at_once, span, channels)
        bias_input = layer_norm(updated.astype(F32)).astype(BF16)
        head_rows = dot_nt(wpb_t, bias_input).astype(BF16).astype(F32)
        for i in range(at_once):
            at = ((chunk // pieces) * at_once + i, slice(None), col)
            bias[at] = bias[at] + head_rows[:, i * span : (i + 1) * span]

    chunks = (local // at_once) * pieces
    def answer():
        @pl.when(is_middle)
        def _():
            blocks(FRINGE, late_sem).wait_recv()
            repeat(FRINGE, lambda step: send(last + step, recv_sem))

    def pair_work(answer=lambda: None):
        for load in loads[1:11]:
            load.wait()
        at = lax.broadcasted_iota(jnp.int32, (local, tokens), 1)
        own_at = lax.broadcasted_iota(jnp.int32, (local, tokens), 0) + me * local
        res_all = res[...].astype(F32)
        chain_all = chain[...].astype(F32)
        here = at == own_at
        own_res = jnp.sum(jnp.where(here, res_all, 0.0), axis=1, keepdims=True)
        own_chain = jnp.sum(jnp.where(here, chain_all, 0.0), axis=1, keepdims=True)
        bins = jnp.where(
            own_chain == chain_all,
            jnp.clip(own_res - res_all + RELMAX, 0.0, 2.0 * RELMAX),
            2.0 * RELMAX + 1.0,
        ).astype(jnp.int32)
        table_t = jnp.concatenate(
            [table[...], jnp.zeros((HEADS, CLASSES - BINS), F32)], axis=1
        )
        high = table_t.astype(BF16)
        rest = table_t - high.astype(F32)
        middle = rest.astype(BF16)
        low = (rest - middle.astype(F32)).astype(BF16)
        classes = lax.broadcasted_iota(jnp.int32, (CLASSES, tokens), 0)
        for r in range(local):
            hot = jnp.where(classes == bins[r : r + 1, :], 1.0, 0.0).astype(BF16)
            bias[r] = dot(high, hot) + (dot(middle, hot) + dot(low, hot))

        half_wa = wa[...] * BF16(0.5)
        wpb_t = wpb[...]

        if chunks <= 8:
            for chunk in range(chunks):
                if chunk == chunks - 1:
                    answer()
                transition(chunk, half_wa, wpb_t)
        else:

            def body(chunk, carry):
                transition(chunk, half_wa, wpb_t)
                return carry

            lax.fori_loop(0, chunks, body, 0)
            answer()

    pl.when(is_early)(pair_work)

    @pl.when(is_late)
    def _():
        pl.semaphore_wait(barrier, devices - 1)
        send(0, late_sem)
        repeat(4, lambda step: send(FRINGE + step, late_sem))
        send(1, late_sem)
        repeat(last - FRINGE - 4, lambda step: send(FRINGE + 4 + step, late_sem))
        repeat(FRINGE - 1, lambda step: send(last + other(me - last, step, FRINGE), late_sem))

    @pl.when(is_middle)
    def _():
        pl.semaphore_wait(barrier, last - 1)
        send(0, recv_sem)
        send(1, recv_sem)
        repeat(last - 1 - FRINGE, lambda step: send(other(me, last - 2 - step, devices), recv_sem))

    @pl.when(is_early)
    def _():
        pl.semaphore_wait(barrier, devices - 1)
        repeat(FRINGE, lambda step: send(last + step, recv_sem))
        repeat(last - 1, lambda step: send(other(me, step, devices), recv_sem))

    pl.when(jnp.logical_not(is_early))(lambda: pair_work(answer))

    loads[11].wait()
    own = layer_norm(single[...].astype(F32)).astype(BF16)
    queries = dot(own, wp[:, :width]).astype(BF16).astype(F32)
    gates = dot(own, wp[:, 3 * width :]).astype(BF16).astype(F32)
    gates_ref[...] = jax.nn.sigmoid(gates)
    values_t = wp[:, 2 * width : 3 * width].astype(F32).T.astype(BF16)
    stack_ref[HEADS * local :, :] = values_t
    mine = own_columns(local, width)
    spread_queries = jnp.where(mine, queries[None, :, :], 0.0)
    spread_queries = spread_queries.reshape(HEADS * local, width).astype(BF16)
    spread_queries = dot_nt(spread_queries, wp[:, width : 2 * width]) * (
        1.0 / math.sqrt(HEAD_DIM)
    )
    stack_ref[: HEADS * local, :] = spread_queries.astype(BF16)
    for i in range(local):
        bias_ref[:, i, :] = bias[i]

    @pl.when(is_middle)
    def _():
        blocks(last - 1, recv_sem).wait_recv()

    @pl.when(is_late)
    def _():
        blocks(FRINGE - 1, late_sem).wait_recv()
        blocks(last, recv_sem).wait_recv()

    @pl.when(is_early)
    def _():
        blocks(last - 1, recv_sem).wait_recv()
        blocks(FRINGE, late_sem).wait_recv()

    blocks(devices - 1, recv_sem).wait_send()


def attention(
    new_pair_from,
    bias,
    keys,
    stack,
    gates,
    mask,
    wo,
    new_pair_ref,
    update_ref,
    update,
    out_sem,
    update_sem,
):
    local, width = gates.shape
    tokens = keys.shape[0]
    out = pltpu.make_async_copy(new_pair_from, new_pair_ref, out_sem)
    out.start()
    both = dot_nt(stack[...], keys[...])
    scores = both[: HEADS * local] + bias[...].reshape(HEADS * local, tokens)
    scores = jnp.where(mask[...] > 0, scores, -1000000000.0)
    expons = jnp.exp(scores - jnp.max(scores, axis=1, keepdims=True)).astype(BF16)
    values_t = both[HEADS * local :].astype(BF16)
    ones = jnp.ones((LANES, tokens), BF16)
    column = lax.broadcasted_iota(jnp.int32, (local, LANES), 1)
    pieces = []
    for first in range(0, width, LANES):
        heads = range(first // HEAD_DIM, -(-(first + LANES) // HEAD_DIM))
        spread = dot_nt(
            expons[heads[0] * local : (heads[-1] + 1) * local],
            jnp.concatenate([values_t[first : first + LANES], ones], axis=0),
        )
        own = spread[:local]
        for at, head in enumerate(heads[1:], 1):
            part = spread[at * local : (at + 1) * local]
            reached = jnp.concatenate([column, column], axis=1) >= head * HEAD_DIM - first
            own = jnp.where(reached, part, own)
        piece = own[:, :LANES] / own[:, LANES:]
        pieces.append(piece)
    attended = jnp.concatenate(pieces, axis=1)
    gated = (gates[...] * attended).astype(BF16)
    update[...] = dot(gated, wo[...]).astype(BF16)
    done = pltpu.make_async_copy(update, update_ref, update_sem)
    done.start()
    done.wait()
    pltpu.make_async_copy(new_pair_from, new_pair_ref, out_sem).wait()


def on_device(
    devices,
    pair,
    single,
    token_mask,
    chain_index,
    residue_index,
    pair_gain,
    pair_norm_offset,
    w_swish_a,
    w_swish_b,
    w_trans_out,
    w_pair_bias,
    w_project,
    w_out,
    relative_position_bias,
):
    def line(vector):
        return vector.reshape(1, vector.shape[0])

    operands = (
        pair,
        single,
        line(chain_index),
        line(residue_index),
        line(pair_gain),
        line(pair_norm_offset),
        w_swish_a,
        w_swish_b,
        w_trans_out,
        w_pair_bias.T,
        w_project,
        relative_position_bias.T,
    )
    local, tokens, _ = pair.shape
    width = single.shape[1]
    anywhere = pl.BlockSpec(memory_space=pl.ANY)
    vmem = pl.BlockSpec(memory_space=pltpu.VMEM)
    held = [
        pltpu.VMEM(pair.shape, pair.dtype),
        pltpu.VMEM(single.shape, single.dtype),
        pltpu.VMEM((local, HEADS, tokens), F32),
    ]
    held += [pltpu.VMEM(x.shape, x.dtype) for x in operands[2:]]
    operands = [pltpu.with_memory_space_constraint(x, pltpu.HBM) for x in operands]
    handed = pl.pallas_call(
        functools.partial(kernel, devices),
        out_shape=(
            jax.ShapeDtypeStruct(pair.shape, BF16),
            jax.ShapeDtypeStruct((HEADS, local, tokens), F32),
            jax.ShapeDtypeStruct((tokens, width), BF16),
            jax.ShapeDtypeStruct((HEADS * local + width, width), BF16),
            jax.ShapeDtypeStruct((local, width), F32),
        ),
        in_specs=[anywhere] * len(operands),
        out_specs=(vmem,) * 5,
        scratch_shapes=held
        + [
            pltpu.SemaphoreType.DMA((3,)),
            pltpu.SemaphoreType.DMA,
            pltpu.SemaphoreType.DMA,
            pltpu.SemaphoreType.DMA,
        ],
        compiler_params=pltpu.CompilerParams(
            collective_id=0, has_side_effects=True, vmem_limit_bytes=GRANT
        ),
        name="pair_tail",
    )(*operands)
    return pl.pallas_call(
        attention,
        out_shape=(
            jax.ShapeDtypeStruct(pair.shape, BF16),
            jax.ShapeDtypeStruct(single.shape, BF16),
        ),
        in_specs=[anywhere] + [vmem] * 6,
        out_specs=(anywhere, anywhere),
        scratch_shapes=[pltpu.VMEM(single.shape, BF16), pltpu.SemaphoreType.DMA, pltpu.SemaphoreType.DMA],
        compiler_params=pltpu.CompilerParams(vmem_limit_bytes=GRANT),
        name="single_attention",
    )(*handed, line(token_mask), w_out)


def solution(mesh):
    rows = P(("groups", "row"))
    return jax.shard_map(
        functools.partial(on_device, mesh.shape["row"]),
        mesh=mesh,
        in_specs=(rows, rows) + (P("groups"),) * 3 + (P(),) * 9,
        out_specs=(rows, rows),
        check_vma=False,
    )
```
